32 devices in a mesh: gx: 8 (over y, x, core), gy: 4 (over z).
Axes of the slice: x: 2, y: 2, z: 4, core: 2. Of those that a mesh axis runs over, the one named last changes fastest.
Arguments:
- object_field: float32 [2, 2048, 4096], P(None, 'gy', 'gx'), may hold values from -6 to 6
- probe: float32 [3, 2, 256, 256], replicated, may hold values from -6 to 6
- positions: int32 [4, 8, 4, 2], P('gy', 'gx'), may hold values from 0 to 512
- frame_count: int32 [4, 8], P('gy', 'gx'), may hold values from 1 to 4, as said below
- measured: float32 [4, 8, 4, 256, 256], P('gy', 'gx'), may hold values from 0.5 to 20
Outputs:
- object_grad: float32 [2, 2048, 4096], P(None, 'gy', 'gx')
The draws below stay inside these ranges and needn't reach their ends.
Inputs may be any that keep to these rules, and one draw needn't show every extreme that they name: `frame_count`: some tile has all 4 slots live in every draw; live frames fill the first slots of a tile; tiles in the columns tx >= 4 have exactly 1 live frame.
All inputs are finite; a program needn't handle non-finite values.
Results may differ from the reference program's by a relative error of at most 0.0045.
Values sent between devices are 32-bit elements; how exact they have to be, the bound alone decides.
No kernel may reach another device: no remote copies, remote signals or barrier semaphores. Data moves between devices by JAX's collectives and lax.ppermute only.
A program may use at most 64 MiB of HBM per device.

```python
import math
import jax
import jax.numpy as jnp
from jax import lax

W = 256
MODES = 3
TILE = 512
HALO = 128
SLOTS = 4
NR = 2048
NC = 4096
N_GX = 8
N_GY = 4


def draw_frame_count(key, part):
    first, second, third, fourth = jax.random.split(jax.random.fold_in(key, 17), 4)
    light = jax.random.randint(first, (N_GY, N_GX), 1, SLOTS // 2 + 1)
    heavy = jax.random.randint(second, (N_GY, N_GX), 0, 2) == 0
    sparse = jax.random.randint(fourth, (N_GY, N_GX), 1, SLOTS // 4 + 1)
    column = jnp.arange(N_GX, dtype=jnp.int32)[None, :]
    left_side = column < N_GX // 2
    counted = jnp.where(left_side, jnp.where(heavy, SLOTS, light), sparse)
    chosen_row = jax.random.randint(third, (), 0, N_GY)
    chosen_col = jax.random.randint(jax.random.fold_in(third, 5), (), 0, N_GX // 2)
    counted = counted.at[chosen_row, chosen_col].set(SLOTS)
    return counted.astype(jnp.int32)


def with_ends(entries, key, least, top_value):
    extent = entries.shape
    spot = [jax.random.randint(jax.random.fold_in(key, axis), (), 0, extent[axis]) for axis in range(len(extent))]
    entries = entries.at[tuple(spot)].set(least)
    longest = extent.index(max(extent))
    spot[longest] = (spot[longest] + 1) % extent[longest]
    return entries.at[tuple(spot)].set(top_value)


def shard_levels(stream_key, dims, pieces, least, top_value):
    loudness = 1.0
    for position, blocks in pieces:
        draws = jax.random.uniform(jax.random.fold_in(jax.random.fold_in(stream_key, 6), position), (blocks,), jnp.float32, least / len(pieces), top_value / len(pieces))
        loudness = loudness * jnp.repeat(jnp.exp(draws), dims[position] // blocks).reshape((-1,) + (1,) * (len(dims) - 1 - position))
    return loudness


def scatter_about(rng, dims, spread, limit, cuts=(), kind=jnp.bfloat16):
    array = jax.random.normal(rng, dims, jnp.float32) * spread
    if len(cuts) > 0:
        array = shard_levels(rng, dims, cuts, -0.22, 0.18) * array
    return jnp.clip(array, min=-limit, max=limit).astype(kind)


def setup_inputs(seed: int = 0) -> dict:
    splits = jax.random.split(jax.random.key(seed), 6)
    return {
        "object_field": scatter_about(splits[0], (2, NR, NC), 1.0, 6.0, ((1, 4), (2, 8)), jnp.float32),
        "probe": scatter_about(splits[1], (MODES, 2, W, W), 1.0, 6.0, (), jnp.float32),
        "positions": with_ends(jax.random.randint(splits[2], (N_GY, N_GX, SLOTS, 2), 0, TILE - W + 2 * HALO + 1), jax.random.fold_in(splits[2], 1), 0, TILE - W + 2 * HALO).astype(jnp.int32),
        "frame_count": draw_frame_count(jax.random.fold_in(splits[5], 71), 0),
        "measured": jnp.clip(jnp.exp(math.log(20.0) - 3.6888795 * jax.random.uniform(splits[4], (N_GY, N_GX, SLOTS, W, W), jnp.float32) ** shard_levels(splits[4], (N_GY, N_GX, SLOTS, W, W), ((0, 4), (1, 8)), -0.2, 0.2)), 0.5, 20.0),
    }


def dft_table(width, sign):
    index = jnp.arange(width, dtype=jnp.float32)
    phase = 2.0 * math.pi / width * jnp.mod(jnp.outer(index, index), width)
    scale = 1.0 / math.sqrt(width)
    cosine = jnp.cos(phase) * scale
    imag_part = sign * jnp.sin(phase) * scale
    upper = jnp.concatenate([cosine, imag_part], axis=1)
    lower = jnp.concatenate([-imag_part, cosine], axis=1)
    return jnp.concatenate([upper, lower], axis=0).astype(jnp.bfloat16)

def apply_rows(real_part, imag_part, table):
    modes, rows, width = real_part.shape
    joined = jnp.concatenate([real_part, imag_part], axis=-1).reshape(modes * rows, 2 * width)
    result = jnp.dot(joined, table, preferred_element_type=jnp.float32).reshape(modes, rows, 2 * width)
    return (result[..., :width], result[..., width:])

def frame_grad(patch, probe, measure, forward, inverse):
    probe_re = probe[:, 0]
    probe_im = probe[:, 1]
    psi_re = (probe_re * patch[0] - probe_im * patch[1]).astype(jnp.bfloat16)
    psi_im = (probe_re * patch[1] + probe_im * patch[0]).astype(jnp.bfloat16)
    half_re, half_im = apply_rows(psi_re, psi_im, forward)
    half_re = jnp.swapaxes(half_re.astype(jnp.bfloat16), 1, 2)
    half_im = jnp.swapaxes(half_im.astype(jnp.bfloat16), 1, 2)
    wave_re, wave_im = apply_rows(half_re, half_im, forward)
    inten = lax.optimization_barrier(jnp.sum(wave_re * wave_re + wave_im * wave_im, axis=0))
    factor = 1.0 - jnp.sqrt(measure).T / jnp.sqrt(inten + 1.0)
    resid_re = (factor * wave_re).astype(jnp.bfloat16)
    resid_im = (factor * wave_im).astype(jnp.bfloat16)
    back_re, back_im = apply_rows(resid_re, resid_im, inverse)
    back_re = jnp.swapaxes(back_re.astype(jnp.bfloat16), 1, 2)
    back_im = jnp.swapaxes(back_im.astype(jnp.bfloat16), 1, 2)
    chi_re, chi_im = apply_rows(back_re, back_im, inverse)
    grad_re = lax.optimization_barrier(jnp.sum(probe_re * chi_re + probe_im * chi_im, axis=0))
    grad_im = lax.optimization_barrier(jnp.sum(probe_re * chi_im - probe_im * chi_re, axis=0))
    return jnp.stack([grad_re, grad_im])

def reference(object_field, probe, positions, frame_count, measured):
    forward = dft_table(W, -1.0)
    inverse = dft_table(W, 1.0)
    padded = jnp.pad(object_field, ((0, 0), (HALO, HALO), (HALO, HALO)))
    zero = jnp.zeros((), jnp.int32)

    def one_tile(index, total):
        row_tile = (index // N_GX).astype(jnp.int32)
        col_tile = (index % N_GX).astype(jnp.int32)
        spots = positions[row_tile, col_tile]
        frames = measured[row_tile, col_tile]

        def one_frame(slot, acc):
            row = (row_tile * TILE + spots[slot, 0]).astype(jnp.int32)
            col = (col_tile * TILE + spots[slot, 1]).astype(jnp.int32)
            patch = lax.dynamic_slice(padded, (zero, row, col), (2, W, W))
            grad = frame_grad(patch, probe, frames[slot], forward, inverse)
            old = lax.dynamic_slice(acc, (zero, row, col), (2, W, W))
            return lax.dynamic_update_slice(acc, old + grad, (zero, row, col))
        return lax.fori_loop(0, frame_count[row_tile, col_tile], one_frame, total)
    total = lax.fori_loop(0, N_GY * N_GX, one_tile, jnp.zeros_like(padded))
    return total[:, HALO:HALO + NR, HALO:HALO + NC]
```

```python
import functools
import math

import jax
import jax.numpy as jnp
import numpy as np
from jax import lax
from jax.experimental import pallas as pl
from jax.experimental.pallas import tpu as pltpu
from jax.sharding import PartitionSpec as P

HALO = 128
LANE = 128
F32 = jnp.float32
BF16 = jnp.bfloat16
ANY = pl.BlockSpec(memory_space=pl.ANY)
VM = pl.BlockSpec(memory_space=pltpu.VMEM)
SM = pl.BlockSpec(memory_space=pltpu.SMEM)


def dft_tables(width):
    half = width // 2
    t = np.arange(width)
    order = np.concatenate([t[0::2], t[1::2]])
    phase = 2.0 * math.pi / width * np.mod(np.outer(t, order), width)
    c = np.cos(phase) / math.sqrt(width)
    s = np.sin(phase) / math.sqrt(width)
    blocks, small = [], []
    for b in (slice(0, half), slice(half, width)):
        blocks += [np.concatenate([c[:, b], s[:, b]]), np.concatenate([-s[:, b], c[:, b]])]
        ct, st = c[:half, b].T, s[:half, b].T
        small.append(np.block([[ct, st], [-st, ct]]))
    fwd = np.concatenate(blocks, axis=1)
    big = np.stack([fwd, fwd.T])
    small = np.stack(small + [m.T for m in small])
    return jnp.asarray(big, BF16), jnp.asarray(small, BF16)


def dot(a, b):
    return jnp.dot(a, b, preferred_element_type=F32)


def prepare_kernel(measured, out):
    slots, width, _ = measured.shape
    half = width // 2
    i = lax.broadcasted_iota(jnp.int32, (width, width), 0)
    j = lax.broadcasted_iota(jnp.int32, (width, width), 1)
    source = jnp.where(j < half, 2 * j, 2 * (j - half) + 1)
    cols = (i == source).astype(F32)
    source = jnp.where(i < half, 2 * i, 2 * (i - half) + 1)
    rows = (j == source).astype(F32)
    for k in range(slots):
        a = jnp.sqrt(measured[k])
        a = jnp.dot(rows, a, precision=lax.Precision.HIGHEST, preferred_element_type=F32)
        out[k] = jnp.dot(a, cols, precision=lax.Precision.HIGHEST, preferred_element_type=F32)


def one_frame(slot, pos, ext, acc, probe, amp, big, small, patch, x, y, xa, xb, u, v, wave, factor):
    modes, _, width, _ = probe.shape
    h = width // 2
    chunk = 64
    lo, hi = slice(0, h), slice(h, width)
    r = pos[slot, 0]
    c = pos[slot, 1]
    q = jnp.minimum(c // LANE, ext.shape[1] - 3)
    s = c - q * LANE
    left = jnp.bitwise_and(LANE - s, LANE - 1)
    right = jnp.bitwise_and(s, LANE - 1)
    lane = lax.broadcasted_iota(jnp.int32, (chunk, LANE), 1)
    keep = lane < LANE - s
    for ch in range(2):
        for i in range(0, width, chunk):
            rows = pl.ds(r + i, chunk)
            rot = [pltpu.roll(ext[ch, q + t, rows, :], left, 1) for t in range(3)]
            patch[ch, i : i + chunk, lo] = jnp.where(keep, rot[0], rot[1])
            patch[ch, i : i + chunk, hi] = jnp.where(keep, rot[1], rot[2])
    for m in range(modes):
        for i in range(0, width, chunk):
            rows = slice(i, i + chunk)
            for cc in (lo, hi):
                pr, pi = probe[m, 0, rows, cc], probe[m, 1, rows, cc]
                o_re, o_im = patch[0, rows, cc], patch[1, rows, cc]
                x[m, rows, cc] = (pr * o_re - pi * o_im).astype(BF16)
                x[m, rows, slice(width + cc.start, width + cc.stop)] = (pr * o_im + pi * o_re).astype(BF16)
        for k in range(2):
            e = dot(x[m], big[0, :, k * width : (k + 1) * width])
            y[m, 0:width, k * h : (k + 1) * h] = e[:, lo].astype(BF16)
            y[m, width:, k * h : (k + 1) * h] = e[:, hi].astype(BF16)
    for m in range(modes):
        for k in range(2):
            p = dot(big[1, k * width : (k + 1) * width], y[m])
            wave[m, k] = p
            square = p[lo] * p[lo] + p[hi] * p[hi]
            factor[k] = square if m == 0 else factor[k] + square
    for k in range(2):
        factor[k] = 1.0 - amp[slot, k * h : (k + 1) * h, :] * lax.rsqrt(factor[k] + 1.0)
    for m in range(modes):
        for k in range(2):
            f = factor[k]
            for part in (lo, hi):
                w = f * wave[m, k, part, :]
                xa[m, k * h : (k + 1) * h, part] = w[:, lo].astype(BF16)
                xb[m, k * h : (k + 1) * h, part] = w[:, hi].astype(BF16)
    for m in range(modes):
        a, b = dot(xa[m], small[0]), dot(xb[m], small[1])
        for cc, z in ((lo, a + b), (hi, a - b)):
            for part in (lo, hi):
                u[m, part, cc] = z[lo, part].astype(BF16)
                v[m, part, cc] = z[hi, part].astype(BF16)
    for m in range(modes):
        a, b = dot(small[2], u[m]), dot(small[3], v[m])
        for rows, z in ((lo, a + b), (hi, a - b)):
            pr, pi = probe[m, 0, rows, :], probe[m, 1, rows, :]
            g_re = pr * z[lo] + pi * z[hi]
            g_im = pr * z[hi] - pi * z[lo]
            if m > 0:
                g_re = g_re + patch[0, rows, :]
                g_im = g_im + patch[1, rows, :]
            patch[0, rows, :] = g_re
            patch[1, rows, :] = g_im
    first = lane < s
    for ch in range(2):
        for i in range(0, width, chunk):
            rows = pl.ds(r + i, chunk)
            g0 = pltpu.roll(patch[ch, i : i + chunk, lo], right, 1)
            g1 = pltpu.roll(patch[ch, i : i + chunk, hi], right, 1)
            zero = jnp.zeros_like(g0)
            acc[ch, q, rows, :] += jnp.where(first, zero, g0)
            acc[ch, q + 1, rows, :] += jnp.where(first, g0, g1)
            acc[ch, q + 2, rows, :] += jnp.where(first, g1, zero)


def frames_kernel(pos, count, here, own, up, down, in_e, in_oa, in_ob, c_e, c_oa, c_ob, probe, amp, big, small,
                  acc, ext, patch, x, y, xa, xb, u, v, wave, factor, sem):
    border = HALO
    rows = own.shape[1]
    blocks = own.shape[2] // LANE
    odd, late = here[0, 0], here[0, 1]
    col_e = jnp.where(odd == 1, 0, blocks + 1)
    col_o = jnp.where(odd == 1, blocks + 1, 0)
    top, mid, low = pl.ds(0, border), pl.ds(border, rows), pl.ds(border + rows, border)
    copies = []
    for b in range(blocks):
        lanes = pl.ds(b * LANE, LANE)
        copies.append((own.at[:, :, lanes], ext.at[:, b + 1, mid]))
        copies.append((up.at[:, :, lanes], ext.at[:, b + 1, top]))
        copies.append((down.at[:, :, lanes], ext.at[:, b + 1, low]))
    copies.append((in_e, ext.at[:, col_e, mid]))
    copies.append((c_e.at[0], ext.at[:, col_e, top]))
    copies.append((c_e.at[1], ext.at[:, col_e, low]))
    ends = (ext.at[:, col_o, mid], ext.at[:, col_o, top], ext.at[:, col_o, low])
    copies = [pltpu.make_async_copy(a, b, sem.at[i]) for i, (a, b) in enumerate(copies)]
    n = len(copies)
    for cp in copies:
        cp.start()

    def outer(strip, corner):
        return [pltpu.make_async_copy(a, b, sem.at[n + i]) for i, (a, b) in enumerate(zip((strip, corner.at[0], corner.at[1]), ends))]

    @pl.when(late == 0)
    def _():
        for cp in outer(in_oa, c_oa):
            cp.start()

    @pl.when(late == 1)
    def _():
        for cp in outer(in_ob, c_ob):
            cp.start()

    acc[...] = jnp.zeros_like(acc)
    for cp in copies + outer(in_oa, c_oa):
        cp.wait()

    def step(slot, carry):
        one_frame(slot, pos, ext, acc, probe, amp, big, small, patch, x, y, xa, xb, u, v, wave, factor)
        return carry

    lax.fori_loop(0, count[0, 0], step, 0)


def rims_kernel(here, acc, in_e, to_up, to_down):
    blocks = acc.shape[1] - 2
    rows = acc.shape[2]
    odd = here[0, 0]
    block_e = jnp.where(odd == 1, 0, blocks - 1)
    top, low = slice(0, HALO), slice(rows - HALO, rows)
    to_up[...] = acc[:, 1 : blocks + 1, top, :]
    to_down[...] = acc[:, 1 : blocks + 1, low, :]
    for ch in range(2):
        to_up[ch, block_e] += in_e[ch, top]
        to_down[ch, block_e] += in_e[ch, low]


def join_kernel(here, acc, in_e, in_oa, in_ob, from_above, from_below, c_above, c_below, out, buf, sem):
    blocks = acc.shape[1] - 2
    rows = acc.shape[2] - 2 * HALO
    odd, late = here[0, 0], here[0, 1]
    block_e = jnp.where(odd == 1, 0, blocks - 1)
    block_o = jnp.where(odd == 1, blocks - 1, 0)
    top, low = slice(0, HALO), slice(rows - HALO, rows)
    for b in range(blocks):
        buf[:, b] = acc[:, b + 1, HALO : HALO + rows, :]
        buf[:, b, top] += from_above[:, b]
        buf[:, b, low] += from_below[:, b]
    for ch in range(2):
        buf[ch, block_e] += in_e[ch, HALO : HALO + rows]
        buf[ch, block_o, top] += c_above[ch]
        buf[ch, block_o, low] += c_below[ch]

    @pl.when(late == 0)
    def _():
        for ch in range(2):
            buf[ch, block_o] += in_oa[ch]

    @pl.when(late == 1)
    def _():
        for ch in range(2):
            buf[ch, block_o] += in_ob[ch]

    copies = [pltpu.make_async_copy(buf.at[:, b], out.at[:, :, pl.ds(b * LANE, LANE)], sem.at[b]) for b in range(blocks)]
    for cp in copies:
        cp.start()
    for cp in copies:
        cp.wait()


def call(kernel, in_specs, out_specs, out_shape, scratch=(), limit=8 << 20, flops=0, moved=0):
    return pl.pallas_call(
        kernel,
        in_specs=in_specs,
        out_specs=out_specs,
        out_shape=out_shape,
        scratch_shapes=scratch,
        compiler_params=pltpu.CompilerParams(vmem_limit_bytes=limit),
        cost_estimate=pl.CostEstimate(flops=flops, bytes_accessed=moved, transcendentals=0),
    )


def body(object_field, probe, positions, frame_count, measured):
    width = probe.shape[-1]
    modes = probe.shape[0]
    _, rows, cols = object_field.shape
    slots = measured.shape[2]
    blocks = cols // LANE
    n_gx = lax.axis_size("gx")
    n_gy = lax.axis_size("gy")
    me = lax.axis_index("gx")
    odd = me % 2
    here = jnp.stack([odd, (me >= n_gx // 2).astype(jnp.int32)]).reshape(1, 2)
    pairs_e = [(i, i ^ 1) for i in range(n_gx) if i ^ 1 < n_gx]
    pairs_o = [(i, i + 1) for i in range(1, n_gx - 1, 2)]
    pairs_o += [(j, i) for i, j in pairs_o]
    pairs_oa = [(i, j) for i, j in pairs_o if j < n_gx // 2]
    pairs_ob = [(i, j) for i, j in pairs_o if j >= n_gx // 2]
    pairs_down = [(i, i + 1) for i in range(n_gy - 1)]
    pairs_up = [(j, i) for i, j in pairs_down]
    shape = functools.partial(jax.ShapeDtypeStruct, dtype=F32)
    zero = jnp.zeros((), jnp.int32)
    far = cols - HALO

    big, small = dft_tables(width)
    up = lax.ppermute(object_field[:, rows - HALO :, :], "gy", pairs_down)
    down = lax.ppermute(object_field[:, :HALO, :], "gy", pairs_up)
    start_e = jnp.where(odd == 1, 0, far)
    start_o = jnp.where(odd == 1, far, 0)

    def edge(array, start):
        return lax.dynamic_slice(array, (zero, zero, start), (2, array.shape[1], HALO))

    mine_e, mine_o = edge(object_field, start_e), edge(object_field, start_o)
    in_e = lax.ppermute(mine_e, "gx", pairs_e)
    in_oa = lax.ppermute(mine_o, "gx", pairs_oa)
    in_ob = lax.ppermute(mine_o, "gx", pairs_ob)
    corner_e = jnp.stack([edge(up, start_e), edge(down, start_e)])
    corner_o = jnp.stack([edge(up, start_o), edge(down, start_o)])
    c_e = lax.ppermute(corner_e, "gx", pairs_e)
    c_oa = lax.ppermute(corner_o, "gx", pairs_oa)
    c_ob = lax.ppermute(corner_o, "gx", pairs_ob)

    amp = call(prepare_kernel, [VM], VM, shape(measured.shape[2:]))(measured[0, 0])

    scratch = pltpu.VMEM
    ext_shape = (2, blocks + 2, rows + 2 * HALO, LANE)
    acc = call(
        frames_kernel,
        [SM] * 3 + [ANY] * 9 + [VM] * 4,
        VM,
        shape(ext_shape),
        [
            scratch(ext_shape, F32),
            scratch((2, width, width), F32),
            scratch((modes, width, 2 * width), BF16),
            scratch((modes, 2 * width, width), BF16),
            scratch((modes, width, width), BF16),
            scratch((modes, width, width), BF16),
            scratch((modes, width, width), BF16),
            scratch((modes, width, width), BF16),
            scratch((modes, 2, width, width), F32),
            scratch((2, width // 2, width), F32),
            pltpu.SemaphoreType.DMA((3 * blocks + 6,)),
        ],
        limit=32 << 20,
        flops=10**10,
        moved=10**7,
    )(positions[0, 0], frame_count, here, object_field, up, down, in_e, in_oa, in_ob, c_e, c_oa, c_ob, probe, amp, big, small)

    col_e = jnp.where(odd == 1, 0, blocks + 1)
    col_o = jnp.where(odd == 1, blocks + 1, 0)
    rim_e = lax.dynamic_index_in_dim(acc, col_e, 1, keepdims=False)
    rim_o = lax.dynamic_index_in_dim(acc, col_o, 1, keepdims=False)
    rim_c = jnp.stack([rim_o[:, :HALO], rim_o[:, -HALO:]])
    rim_o = rim_o[:, HALO:-HALO]
    back_e = lax.ppermute(rim_e, "gx", pairs_e)
    back_ca = lax.ppermute(rim_c, "gx", pairs_oa)
    back_cb = lax.ppermute(rim_c, "gx", pairs_ob)
    back_c = back_ca + back_cb
    strip = shape((2, blocks, HALO, LANE))
    to_up, to_down = call(rims_kernel, [SM, VM, VM], [VM, VM], [strip, strip])(here, acc, back_e)
    from_below = lax.ppermute(to_up, "gy", pairs_up)
    from_above = lax.ppermute(to_down, "gy", pairs_down)
    back_oa = lax.ppermute(rim_o, "gx", pairs_oa)
    back_ob = lax.ppermute(rim_o, "gx", pairs_ob)
    c_below = lax.ppermute(back_c[0], "gy", pairs_up)
    c_above = lax.ppermute(back_c[1], "gy", pairs_down)
    return call(
        join_kernel,
        [SM] + [VM] * 8,
        ANY,
        shape(object_field.shape),
        [scratch((2, blocks, rows, LANE), F32), pltpu.SemaphoreType.DMA((blocks,))],
        limit=16 << 20,
    )(here, acc, back_e, back_oa, back_ob, from_above, from_below, c_above, c_below)


def solution(mesh):
    return jax.shard_map(
        body,
        mesh=mesh,
        in_specs=(
            P(None, "gy", "gx"),
            P(),
            P("gy", "gx", None, None),
            P("gy", "gx"),
            P("gy", "gx", None, None, None),
        ),
        out_specs=P(None, "gy", "gx"),
        check_vma=False,
    )
```

```python
import functools
import math

import jax
import jax.numpy as jnp
import numpy as np
from jax import lax
from jax.experimental import pallas as pl
from jax.experimental.pallas import tpu as pltpu
from jax.sharding import PartitionSpec as P


HALO = 128
LANE = 128
F32 = jnp.float32
BF16 = jnp.bfloat16
ANY = pl.BlockSpec(memory_space=pl.ANY)
VM = pl.BlockSpec(memory_space=pltpu.VMEM)
SM = pl.BlockSpec(memory_space=pltpu.SMEM)
HB = pl.BlockSpec(memory_space=pltpu.HBM)


def dft_tables(width):
    half = width // 2
    t = np.arange(width)
    order = np.concatenate([t[0::2], t[1::2]])
    phase = 2.0 * math.pi / width * np.mod(np.outer(t, order), width)
    c = np.cos(phase) / math.sqrt(width)
    s = np.sin(phase) / math.sqrt(width)
    blocks, small = [], []
    for b in (slice(0, half), slice(half, width)):
        blocks += [np.concatenate([c[:, b], s[:, b]]), np.concatenate([-s[:, b], c[:, b]])]
        ct, st = c[:half, b].T, s[:half, b].T
        small.append(np.block([[ct, st], [-st, ct]]))
    fwd = np.concatenate(blocks, axis=1)
    big = np.stack([fwd, fwd.T])
    small = np.stack(small + [m.T for m in small])
    return jnp.asarray(big, BF16), jnp.asarray(small, BF16)


def dot(a, b):
    return jnp.dot(a, b, preferred_element_type=F32)


def rows_kernel(own, to_up, to_down, sem):
    rows = own.shape[1]
    copies = [
        pltpu.make_async_copy(own.at[:, pl.ds(rows - HALO, HALO), :], to_down, sem.at[0]),
        pltpu.make_async_copy(own.at[:, pl.ds(0, HALO), :], to_up, sem.at[1]),
    ]
    for cp in copies:
        cp.start()
    for cp in copies:
        cp.wait()


def edges_kernel(info, own, edge_e, edge_o, sem):
    far = own.shape[2] - HALO
    odd = info[0, 0]
    start_e = pl.multiple_of(jnp.where(odd == 1, 0, far), LANE)
    start_o = pl.multiple_of(jnp.where(odd == 1, far, 0), LANE)
    copies = [
        pltpu.make_async_copy(own.at[:, :, pl.ds(start_e, HALO)], edge_e, sem.at[0]),
        pltpu.make_async_copy(own.at[:, :, pl.ds(start_o, HALO)], edge_o, sem.at[1]),
    ]
    for cp in copies:
        cp.start()
    for cp in copies:
        cp.wait()


def corners_kernel(info, up, down, corner_e, corner_o):
    far = up.shape[2] - HALO
    odd = info[0, 0]
    start_e = pl.multiple_of(jnp.where(odd == 1, 0, far), LANE)
    start_o = pl.multiple_of(jnp.where(odd == 1, far, 0), LANE)
    for i, strip in enumerate((up, down)):
        corner_e[i] = strip[:, :, pl.ds(start_e, HALO)]
        corner_o[i] = strip[:, :, pl.ds(start_o, HALO)]


def prepare_kernel(measured_h, own, probe, big, small, amp, ext, acc, probe_v, big_v, small_v, measured, sem):
    slots, width, _ = measured.shape
    half = width // 2
    rows = own.shape[1]
    blocks = own.shape[2] // LANE
    copies = [(measured_h, measured), (probe, probe_v), (big, big_v), (small, small_v)]
    for b in range(blocks):
        copies.append((own.at[:, :, pl.ds(b * LANE, LANE)], ext.at[:, b + 1, pl.ds(HALO, rows)]))
    copies = [pltpu.make_async_copy(p, q, sem.at[i]) for i, (p, q) in enumerate(copies)]
    for cp in copies:
        cp.start()
    acc[...] = jnp.zeros_like(acc)
    i = lax.broadcasted_iota(jnp.int32, (width, width), 0)
    j = lax.broadcasted_iota(jnp.int32, (width, width), 1)
    source = jnp.where(j < half, 2 * j, 2 * (j - half) + 1)
    cols = (i == source).astype(F32)
    source = jnp.where(i < half, 2 * i, 2 * (i - half) + 1)
    perm = (j == source).astype(F32)
    copies[0].wait()
    for k in range(slots):
        a = jnp.sqrt(measured[k])
        a = jnp.dot(perm, a, precision=lax.Precision.HIGHEST, preferred_element_type=F32)
        amp[k] = jnp.dot(a, cols, precision=lax.Precision.HIGHEST, preferred_element_type=F32)
    for cp in copies[1:]:
        cp.wait()


def one_frame(slot, info, ext, acc, probe, amp, big, small, patch, x, y, xa, xb, u, v, wave, factor):
    modes, _, width, _ = probe.shape
    h = width // 2
    chunk = 64
    lo, hi = slice(0, h), slice(h, width)
    r = info[0, 2 + 2 * slot]
    c = info[0, 3 + 2 * slot]
    q = jnp.minimum(c // LANE, ext.shape[1] - 3)
    s = c - q * LANE
    left = jnp.bitwise_and(LANE - s, LANE - 1)
    right = jnp.bitwise_and(s, LANE - 1)
    lane = lax.broadcasted_iota(jnp.int32, (chunk, LANE), 1)
    keep = lane < LANE - s
    for ch in range(2):
        for i in range(0, width, chunk):
            rows = pl.ds(r + i, chunk)
            rot = [pltpu.roll(ext[ch, q + t, rows, :], left, 1) for t in range(3)]
            patch[ch, i : i + chunk, lo] = jnp.where(keep, rot[0], rot[1])
            patch[ch, i : i + chunk, hi] = jnp.where(keep, rot[1], rot[2])
    for m in range(modes):
        for i in range(0, width, chunk):
            rows = slice(i, i + chunk)
            for cc in (lo, hi):
                pr, pi = probe[m, 0, rows, cc], probe[m, 1, rows, cc]
                o_re, o_im = patch[0, rows, cc], patch[1, rows, cc]
                x[m, rows, cc] = (pr * o_re - pi * o_im).astype(BF16)
                x[m, rows, slice(width + cc.start, width + cc.stop)] = (pr * o_im + pi * o_re).astype(BF16)
        for k in range(2):
            e = dot(x[m], big[0, :, k * width : (k + 1) * width])
            y[m, 0:width, k * h : (k + 1) * h] = e[:, lo].astype(BF16)
            y[m, width:, k * h : (k + 1) * h] = e[:, hi].astype(BF16)
    for m in range(modes):
        for k in range(2):
            p = dot(big[1, k * width : (k + 1) * width], y[m])
            wave[m, k] = p
            square = p[lo] * p[lo] + p[hi] * p[hi]
            factor[k] = square if m == 0 else factor[k] + square
    for k in range(2):
        factor[k] = 1.0 - amp[slot, k * h : (k + 1) * h, :] * lax.rsqrt(factor[k] + 1.0)
    for m in range(modes):
        for k in range(2):
            f = factor[k]
            for part in (lo, hi):
                w = f * wave[m, k, part, :]
                xa[m, k * h : (k + 1) * h, part] = w[:, lo].astype(BF16)
                xb[m, k * h : (k + 1) * h, part] = w[:, hi].astype(BF16)
    for m in range(modes):
        a, b = dot(xa[m], small[0]), dot(xb[m], small[1])
        for cc, z in ((lo, a + b), (hi, a - b)):
            for part in (lo, hi):
                u[m, part, cc] = z[lo, part].astype(BF16)
                v[m, part, cc] = z[hi, part].astype(BF16)
    for m in range(modes):
        a, b = dot(small[2], u[m]), dot(small[3], v[m])
        for rows, z in ((lo, a + b), (hi, a - b)):
            pr, pi = probe[m, 0, rows, :], probe[m, 1, rows, :]
            g_re = pr * z[lo] + pi * z[hi]
            g_im = pr * z[hi] - pi * z[lo]
            if m > 0:
                g_re = g_re + patch[0, rows, :]
                g_im = g_im + patch[1, rows, :]
            patch[0, rows, :] = g_re
            patch[1, rows, :] = g_im
    first = lane < s
    for ch in range(2):
        for i in range(0, width, chunk):
            rows = pl.ds(r + i, chunk)
            g0 = pltpu.roll(patch[ch, i : i + chunk, lo], right, 1)
            g1 = pltpu.roll(patch[ch, i : i + chunk, hi], right, 1)
            zero = jnp.zeros_like(g0)
            acc[ch, q, rows, :] += jnp.where(first, zero, g0)
            acc[ch, q + 1, rows, :] += jnp.where(first, g0, g1)
            acc[ch, q + 2, rows, :] += jnp.where(first, g1, zero)


def frame_stage(slot, info, odd, cols, width):
    c = info[0, 3 + 2 * slot]
    needs_right = c > cols + HALO - width
    needs_left = c < HALO
    return jnp.where(jnp.where(odd == 1, needs_right, needs_left), 1, 0)


def run_frames(stage, info, ext, acc, probe, amp, big, small, *scratch):
    width = probe.shape[-1]
    cols = (ext.shape[1] - 2) * LANE

    def step(slot, carry):
        @pl.when(frame_stage(slot, info, info[0, 0], cols, width) == stage)
        def _():
            one_frame(slot, info, ext, acc, probe, amp, big, small, *scratch)

        return carry

    lax.fori_loop(0, info[0, 1], step, 0)


def copy_all(pairs, sem):
    copies = [pltpu.make_async_copy(a, b, sem.at[i]) for i, (a, b) in enumerate(pairs)]
    for cp in copies:
        cp.start()
    for cp in copies:
        cp.wait()


def near_kernel(info, up, down, in_e, c_e, probe, amp, big, small, ext_in, acc_in, ext, acc, *rest):
    *scratch, sem = rest
    blocks = ext.shape[1] - 2
    rows = ext.shape[2] - 2 * HALO
    col_e = jnp.where(info[0, 0] == 1, 0, blocks + 1)
    top, mid, low = pl.ds(0, HALO), pl.ds(HALO, rows), pl.ds(HALO + rows, HALO)
    pairs = []
    for b in range(blocks):
        lanes = pl.ds(b * LANE, LANE)
        pairs.append((up.at[:, :, lanes], ext.at[:, b + 1, top]))
        pairs.append((down.at[:, :, lanes], ext.at[:, b + 1, low]))
    pairs += [(in_e, ext.at[:, col_e, mid]), (c_e.at[0], ext.at[:, col_e, top]), (c_e.at[1], ext.at[:, col_e, low])]
    copy_all(pairs, sem)
    run_frames(0, info, ext, acc, probe, amp, big, small, *scratch)


def outer_kernel(info, in_o, c_o, probe, amp, big, small, ext_in, acc_in,
                 ext, acc, rim_e, rim_o, rim_top, rim_low, *rest):
    *scratch, sem = rest
    blocks = ext.shape[1] - 2
    rows = ext.shape[2] - 2 * HALO
    odd = info[0, 0]
    col_e = jnp.where(odd == 1, 0, blocks + 1)
    col_o = jnp.where(odd == 1, blocks + 1, 0)
    top, mid, low = pl.ds(0, HALO), pl.ds(HALO, rows), pl.ds(HALO + rows, HALO)
    copy_all([(in_o, ext.at[:, col_o, mid]), (c_o.at[0], ext.at[:, col_o, top]), (c_o.at[1], ext.at[:, col_o, low])], sem)
    run_frames(1, info, ext, acc, probe, amp, big, small, *scratch)
    for ch in range(2):
        rim_e[ch] = acc[ch, col_e]
        rim_top[ch] = acc[ch, col_o, 0:HALO]
        rim_o[ch] = acc[ch, col_o, HALO : HALO + rows]
        rim_low[ch] = acc[ch, col_o, HALO + rows :]


def rims_kernel(info, acc, in_e, to_up, to_down):
    blocks = acc.shape[1] - 2
    rows = acc.shape[2]
    odd = info[0, 0]
    block_e = jnp.where(odd == 1, 0, blocks - 1)
    top, low = slice(0, HALO), slice(rows - HALO, rows)
    to_up[...] = acc[:, 1 : blocks + 1, top, :]
    to_down[...] = acc[:, 1 : blocks + 1, low, :]
    for ch in range(2):
        to_up[ch, block_e] += in_e[ch, top]
        to_down[ch, block_e] += in_e[ch, low]


def join_kernel(info, acc, in_e, in_o, from_above, from_below, c_above, c_below, out, buf, sem):
    blocks = acc.shape[1] - 2
    rows = acc.shape[2] - 2 * HALO
    odd = info[0, 0]
    block_e = jnp.where(odd == 1, 0, blocks - 1)
    block_o = jnp.where(odd == 1, blocks - 1, 0)
    top, low = slice(0, HALO), slice(rows - HALO, rows)
    for b in range(blocks):
        buf[:, b] = acc[:, b + 1, HALO : HALO + rows, :]
        buf[:, b, top] += from_above[:, b]
        buf[:, b, low] += from_below[:, b]
    for ch in range(2):
        buf[ch, block_e] += in_e[ch, HALO : HALO + rows]
        buf[ch, block_o] += in_o[ch]
        buf[ch, block_o, top] += c_above[ch]
        buf[ch, block_o, low] += c_below[ch]
    copies = [pltpu.make_async_copy(buf.at[:, b], out.at[:, :, pl.ds(b * LANE, LANE)], sem.at[b]) for b in range(blocks)]
    for cp in copies:
        cp.start()
    for cp in copies:
        cp.wait()


def call(kernel, in_specs, out_specs, out_shape, scratch=(), limit=8 << 20, flops=0, moved=0, aliases=None):
    return pl.pallas_call(
        kernel,
        in_specs=in_specs,
        out_specs=out_specs,
        out_shape=out_shape,
        scratch_shapes=scratch,
        input_output_aliases=aliases or {},
        compiler_params=pltpu.CompilerParams(vmem_limit_bytes=limit),
        cost_estimate=pl.CostEstimate(flops=flops, bytes_accessed=moved, transcendentals=0),
    )


def program(object_field, probe, positions, frame_count, measured):
    width = probe.shape[-1]
    modes = probe.shape[0]
    _, rows, cols = object_field.shape
    blocks = cols // LANE
    n_gx = lax.axis_size("gx")
    n_gy = lax.axis_size("gy")
    slots = measured.shape[2]
    odd = (lax.axis_index("gx") % 2).astype(jnp.int32)
    info = jnp.concatenate([odd.reshape(1), frame_count.reshape(1), positions.reshape(2 * slots)]).reshape(1, -1)
    object_field, probe, measured = [pltpu.with_memory_space_constraint(a, pltpu.HBM) for a in (object_field, probe, measured[0, 0])]
    pairs_e = [(i, i ^ 1) for i in range(n_gx) if i ^ 1 < n_gx]
    pairs_o = [(i, i + 1) for i in range(1, n_gx - 1, 2)]
    pairs_o += [(j, i) for i, j in pairs_o]
    pairs_down = [(i, i + 1) for i in range(n_gy - 1)]
    pairs_up = [(j, i) for i, j in pairs_down]

    def diagonal(pairs):
        return [(i * n_gy + z, j * n_gy + w) for z, w in pairs for i, j in pairs_o]

    shape = functools.partial(jax.ShapeDtypeStruct, dtype=F32)
    vmem = pltpu.VMEM
    dma = pltpu.SemaphoreType.DMA
    big, small = [pltpu.with_memory_space_constraint(a, pltpu.HBM) for a in dft_tables(width)]

    strip = shape((2, HALO, cols))
    to_up, to_down = call(rows_kernel, [HB], [VM] * 2, [strip] * 2, [dma((2,))])(object_field)
    up = lax.ppermute(to_down, "gy", pairs_down)
    down = lax.ppermute(to_up, "gy", pairs_up)
    edge = shape((2, rows, HALO))
    edge_e, edge_o = call(edges_kernel, [SM, HB], [VM] * 2, [edge] * 2, [dma((2,))])(info, object_field)
    in_e = lax.ppermute(edge_e, "gx", pairs_e)
    in_o = lax.ppermute(edge_o, "gx", pairs_o)

    ext_shape = (2, blocks + 2, rows + 2 * HALO, LANE)
    amp, ext, acc, probe, big, small = call(
        prepare_kernel,
        [HB] * 5,
        [VM] * 6,
        [shape(measured.shape), shape(ext_shape), shape(ext_shape), shape(probe.shape),
         jax.ShapeDtypeStruct(big.shape, BF16), jax.ShapeDtypeStruct(small.shape, BF16)],
        [vmem(measured.shape, F32), dma((4 + blocks,))],
        limit=24 << 20,
        flops=10**9,
        moved=10**7,
    )(measured, object_field, probe, big, small)

    corner = shape((2, 2, HALO, HALO))
    corner_e, corner_o = call(corners_kernel, [SM, VM, VM], [VM] * 2, [corner] * 2)(info, up, down)
    c_e = lax.ppermute(corner_e, "gx", pairs_e)
    c_o = lax.ppermute(corner_o, "gx", pairs_o)

    work = [
        vmem((2, width, width), F32),
        vmem((modes, width, 2 * width), BF16),
        vmem((modes, 2 * width, width), BF16),
        vmem((modes, width, width), BF16),
        vmem((modes, width, width), BF16),
        vmem((modes, width, width), BF16),
        vmem((modes, width, width), BF16),
        vmem((modes, 2, width, width), F32),
        vmem((2, width // 2, width), F32),
        dma((2 * blocks + 3,)),
    ]
    ext, acc = call(
        near_kernel,
        [SM] + [ANY] * 4 + [VM] * 6,
        [VM] * 2,
        [shape(ext_shape)] * 2,
        work,
        limit=32 << 20,
        flops=10**10,
        moved=10**7,
        aliases={9: 0, 10: 1},
    )(info, up, down, in_e, c_e, probe, amp, big, small, ext, acc)
    piece = shape((2, HALO, HALO))
    _, acc, rim_e, rim_o, rim_top, rim_low = call(
        outer_kernel,
        [SM] + [ANY] * 2 + [VM] * 6,
        [VM] * 6,
        [shape(ext_shape)] * 2 + [shape((2, rows + 2 * HALO, HALO)), edge, piece, piece],
        work,
        limit=32 << 20,
        flops=10**10,
        moved=10**7,
        aliases={7: 0, 8: 1},
    )(info, in_o, c_o, probe, amp, big, small, ext, acc)

    back_e = lax.ppermute(rim_e, "gx", pairs_e)
    back_o = lax.ppermute(rim_o, "gx", pairs_o)
    strip = shape((2, blocks, HALO, LANE))
    to_up, to_down = call(rims_kernel, [SM, VM, VM], [VM] * 2, [strip] * 2)(info, acc, back_e)
    from_below = lax.ppermute(to_up, "gy", pairs_up)
    from_above = lax.ppermute(to_down, "gy", pairs_down)
    c_below = lax.ppermute(rim_top, ("gx", "gy"), diagonal(pairs_up))
    c_above = lax.ppermute(rim_low, ("gx", "gy"), diagonal(pairs_down))
    return call(
        join_kernel,
        [SM] + [VM] * 7,
        ANY,
        shape(object_field.shape),
        [vmem((2, blocks, rows, LANE), F32), dma((blocks,))],
        limit=16 << 20,
    )(info, acc, back_e, back_o, from_above, from_below, c_above, c_below)


def solution(mesh):
    return jax.shard_map(
        program,
        mesh=mesh,
        in_specs=(
            P(None, "gy", "gx"),
            P(),
            P("gy", "gx", None, None),
            P("gy", "gx"),
            P("gy", "gx", None, None, None),
        ),
        out_specs=P(None, "gy", "gx"),
        check_vma=False,
    )
```

```python
import functools
import math

import jax
import jax.numpy as jnp
import numpy as np
from jax import lax
from jax.experimental import pallas as pl
from jax.experimental.pallas import tpu as pltpu
from jax.sharding import PartitionSpec as P


HALO = 128
LANE = 128
F32 = jnp.float32
BF16 = jnp.bfloat16
ANY = pl.BlockSpec(memory_space=pl.ANY)
VM = pl.BlockSpec(memory_space=pltpu.VMEM)
SM = pl.BlockSpec(memory_space=pltpu.SMEM)
HB = pl.BlockSpec(memory_space=pltpu.HBM)


def dft_tables(width):
    half = width // 2
    t = np.arange(width)
    order = np.concatenate([t[0::2], t[1::2]])
    phase = 2.0 * math.pi / width * np.mod(np.outer(t, order), width)
    c = np.cos(phase) / math.sqrt(width)
    s = np.sin(phase) / math.sqrt(width)
    blocks, small = [], []
    for b in (slice(0, half), slice(half, width)):
        blocks += [np.concatenate([c[:, b], s[:, b]]), np.concatenate([-s[:, b], c[:, b]])]
        ct, st = c[:half, b].T, s[:half, b].T
        small.append(np.block([[ct, st], [-st, ct]]))
    fwd = np.concatenate(blocks, axis=1)
    big = np.stack([fwd, fwd.T])
    small = np.stack(small + [m.T for m in small])
    return jnp.asarray(big, BF16), jnp.asarray(small, BF16)


def dot(a, b):
    return jnp.dot(a, b, preferred_element_type=F32)


def sides(blocks):
    odd = lax.rem(lax.axis_index("gx"), 2) == 1
    return jnp.where(odd, 0, blocks + 1), jnp.where(odd, blocks + 1, 0)


def ends(far):
    odd = lax.rem(lax.axis_index("gy"), 2) == 1
    first, second = jnp.where(odd, 0, far), jnp.where(odd, far, 0)
    return pl.multiple_of(first, HALO), pl.multiple_of(second, HALO)


def rows_kernel(own, first, second, sem):
    offsets = ends(own.shape[1] - HALO)
    copies = [
        pltpu.make_async_copy(own.at[:, pl.ds(at, HALO), :], strip, sem.at[i])
        for i, (at, strip) in enumerate(zip(offsets, (first, second)))
    ]
    for cp in copies:
        cp.start()
    for cp in copies:
        cp.wait()


def edge_kernel(which, own, edge, sem):
    block = sides(own.shape[2] // LANE - 2)[which]
    lanes = pl.ds(pl.multiple_of(block * LANE, LANE), LANE)
    cp = pltpu.make_async_copy(own.at[:, :, lanes], edge, sem.at[0])
    cp.start()
    cp.wait()


def inner_edge_kernel(*refs):
    edge_kernel(0, *refs)


def outer_edge_kernel(*refs):
    edge_kernel(1, *refs)


def corners_kernel(first, second, corner_e, corner_o):
    block_e, block_o = sides(first.shape[2] // LANE - 2)
    for i, strip in enumerate((first, second)):
        corner_e[i] = strip[:, :, pl.ds(pl.multiple_of(block_e * LANE, LANE), LANE)]
        corner_o[i] = strip[:, :, pl.ds(pl.multiple_of(block_o * LANE, LANE), LANE)]


def prepare_kernel(info, measured_h, own, probe, big, small, amp, ext, acc, probe_v, big_v, small_v, measured, sem):
    slots, width, _ = measured.shape
    half = width // 2
    rows = own.shape[1]
    blocks = own.shape[2] // LANE
    copies = [(measured_h, measured), (probe, probe_v), (big, big_v), (small, small_v)]
    for b in range(blocks):
        copies.append((own.at[:, :, pl.ds(b * LANE, LANE)], ext.at[:, b + 1, pl.ds(HALO, rows)]))
    copies = [pltpu.make_async_copy(p, q, sem.at[i]) for i, (p, q) in enumerate(copies)]
    for cp in copies:
        cp.start()
    acc[...] = jnp.zeros_like(acc)
    i = lax.broadcasted_iota(jnp.int32, (width, width), 0)
    j = lax.broadcasted_iota(jnp.int32, (width, width), 1)
    source = jnp.where(j < half, 2 * j, 2 * (j - half) + 1)
    cols = (i == source).astype(F32)
    source = jnp.where(i < half, 2 * i, 2 * (i - half) + 1)
    perm = (j == source).astype(F32)
    copies[0].wait()
    for k in range(slots):
        a = jnp.sqrt(measured[k])
        a = jnp.dot(perm, a, precision=lax.Precision.HIGHEST, preferred_element_type=F32)
        amp[k] = jnp.dot(a, cols, precision=lax.Precision.HIGHEST, preferred_element_type=F32)
    for cp in copies[1:]:
        cp.wait()


def one_frame(slot, info, ext, acc, probe, amp, big, small, patch, x, y, xa, xb, u, v, wave, factor):
    modes, _, width, _ = probe.shape
    h = width // 2
    chunk = 64
    lo, hi = slice(0, h), slice(h, width)
    r = info[0, 1 + 2 * slot]
    c = info[0, 2 + 2 * slot]
    q = jnp.minimum(c // LANE, ext.shape[1] - 3)
    s = c - q * LANE
    left = jnp.bitwise_and(LANE - s, LANE - 1)
    right = jnp.bitwise_and(s, LANE - 1)
    lane = lax.broadcasted_iota(jnp.int32, (chunk, LANE), 1)
    keep = lane < LANE - s
    for ch in range(2):
        for i in range(0, width, chunk):
            rows = pl.ds(r + i, chunk)
            rot = [pltpu.roll(ext[ch, q + t, rows, :], left, 1) for t in range(3)]
            patch[ch, i : i + chunk, lo] = jnp.where(keep, rot[0], rot[1])
            patch[ch, i : i + chunk, hi] = jnp.where(keep, rot[1], rot[2])
    for m in range(modes):
        for i in range(0, width, chunk):
            rows = slice(i, i + chunk)
            for cc in (lo, hi):
                pr, pi = probe[m, 0, rows, cc], probe[m, 1, rows, cc]
                o_re, o_im = patch[0, rows, cc], patch[1, rows, cc]
                x[m, rows, cc] = (pr * o_re - pi * o_im).astype(BF16)
                x[m, rows, slice(width + cc.start, width + cc.stop)] = (pr * o_im + pi * o_re).astype(BF16)
        for k in range(2):
            e = dot(x[m], big[0, :, k * width : (k + 1) * width])
            y[m, 0:width, k * h : (k + 1) * h] = e[:, lo].astype(BF16)
            y[m, width:, k * h : (k + 1) * h] = e[:, hi].astype(BF16)
    for m in range(modes):
        for k in range(2):
            p = dot(big[1, k * width : (k + 1) * width], y[m])
            wave[m, k] = p
            square = p[lo] * p[lo] + p[hi] * p[hi]
            factor[k] = square if m == 0 else factor[k] + square
    for k in range(2):
        factor[k] = 1.0 - amp[slot, k * h : (k + 1) * h, :] * lax.rsqrt(factor[k] + 1.0)
    for m in range(modes):
        for k in range(2):
            f = factor[k]
            for part in (lo, hi):
                w = f * wave[m, k, part, :]
                xa[m, k * h : (k + 1) * h, part] = w[:, lo].astype(BF16)
                xb[m, k * h : (k + 1) * h, part] = w[:, hi].astype(BF16)
    for m in range(modes):
        a, b = dot(xa[m], small[0]), dot(xb[m], small[1])
        for cc, z in ((lo, a + b), (hi, a - b)):
            for part in (lo, hi):
                u[m, part, cc] = z[lo, part].astype(BF16)
                v[m, part, cc] = z[hi, part].astype(BF16)
    for m in range(modes):
        a, b = dot(small[2], u[m]), dot(small[3], v[m])
        for rows, z in ((lo, a + b), (hi, a - b)):
            pr, pi = probe[m, 0, rows, :], probe[m, 1, rows, :]
            g_re = pr * z[lo] + pi * z[hi]
            g_im = pr * z[hi] - pi * z[lo]
            if m > 0:
                g_re = g_re + patch[0, rows, :]
                g_im = g_im + patch[1, rows, :]
            patch[0, rows, :] = g_re
            patch[1, rows, :] = g_im
    first = lane < s
    for ch in range(2):
        for i in range(0, width, chunk):
            rows = pl.ds(r + i, chunk)
            g0 = pltpu.roll(patch[ch, i : i + chunk, lo], right, 1)
            g1 = pltpu.roll(patch[ch, i : i + chunk, hi], right, 1)
            zero = jnp.zeros_like(g0)
            acc[ch, q, rows, :] += jnp.where(first, zero, g0)
            acc[ch, q + 1, rows, :] += jnp.where(first, g0, g1)
            acc[ch, q + 2, rows, :] += jnp.where(first, g1, zero)


def frame_stage(slot, info, cols, width):
    c = info[0, 2 + 2 * slot]
    odd = lax.rem(lax.axis_index("gx"), 2) == 1
    return jnp.where(odd, c > cols + HALO - width, c < HALO).astype(jnp.int32)


def run_frames(stage, info, ext, acc, probe, amp, big, small, *scratch):
    width = probe.shape[-1]
    cols = (ext.shape[1] - 2) * LANE

    def step(slot, carry):
        @pl.when(frame_stage(slot, info, cols, width) == stage)
        def _():
            one_frame(slot, info, ext, acc, probe, amp, big, small, *scratch)

        return carry

    lax.fori_loop(0, info[0, 0], step, 0)


def near_kernel(info, first, second, in_e, c_e, probe, amp, big, small, ext_in, acc_in, ext, acc, *rest):
    blocks = ext.shape[1] - 2
    rows = ext.shape[2] - 2 * HALO
    col_e, _ = sides(blocks)
    for i, (at, strip) in enumerate(zip(ends(HALO + rows), (first, second))):
        for ch in range(2):
            for b in range(blocks):
                ext[ch, b + 1, pl.ds(at, HALO)] = strip[ch, :, b * LANE : (b + 1) * LANE]
            ext[ch, col_e, pl.ds(at, HALO)] = c_e[i, ch]
    for ch in range(2):
        ext[ch, col_e, HALO : HALO + rows] = in_e[ch]
    run_frames(0, info, ext, acc, probe, amp, big, small, *rest)


def outer_kernel(info, in_o, c_o, probe, amp, big, small, ext_in, acc_in,
                 ext, acc, rim_e, rim_o, rim_first, rim_second, *rest):
    blocks = ext.shape[1] - 2
    rows = ext.shape[2] - 2 * HALO
    col_e, col_o = sides(blocks)
    offsets = ends(HALO + rows)
    for ch in range(2):
        for i, at in enumerate(offsets):
            ext[ch, col_o, pl.ds(at, HALO)] = c_o[i, ch]
        ext[ch, col_o, HALO : HALO + rows] = in_o[ch]
    run_frames(1, info, ext, acc, probe, amp, big, small, *rest)
    for ch in range(2):
        rim_e[ch] = acc[ch, col_e]
        for at, rim in zip(offsets, (rim_first, rim_second)):
            rim[ch] = acc[ch, col_o, pl.ds(at, HALO)]
        rim_o[ch] = acc[ch, col_o, HALO : HALO + rows]


def rims_kernel(acc, in_e, first, second):
    blocks = acc.shape[1] - 2
    block_e, _ = sides(blocks - 2)
    for at, strip in zip(ends(acc.shape[2] - HALO), (first, second)):
        for ch in range(2):
            for b in range(blocks):
                strip[ch, b] = acc[ch, b + 1, pl.ds(at, HALO)]
            strip[ch, block_e] += in_e[ch, pl.ds(at, HALO)]


def inner_join_kernel(acc, in_e, first, second, out, buf, sem):
    blocks = acc.shape[1] - 2
    rows = acc.shape[2] - 2 * HALO
    block_e, block_o = sides(blocks - 2)
    start = jnp.where(block_o == 0, 1, 0)
    copies = []
    for t in range(blocks - 1):
        b = start + t
        for ch in range(2):
            buf[ch, t] = acc[ch, b + 1, HALO : HALO + rows, :]
            for at, strip in zip(ends(rows - HALO), (first, second)):
                buf[ch, t, pl.ds(at, HALO)] += strip[ch, b]
    for ch in range(2):
        buf[ch, block_e - start] += in_e[ch, HALO : HALO + rows]
    for t in range(blocks - 1):
        lanes = pl.ds(pl.multiple_of((start + t) * LANE, LANE), LANE)
        copies.append(pltpu.make_async_copy(buf.at[:, t], out.at[:, :, lanes], sem.at[t]))
        copies[-1].start()
    for cp in copies:
        cp.wait()


def outer_join_kernel(acc, in_o, first, second, c_first, c_second, out_in, out, buf, sem):
    blocks = acc.shape[1] - 2
    rows = acc.shape[2] - 2 * HALO
    _, b = sides(blocks - 2)
    for ch in range(2):
        buf[ch] = acc[ch, b + 1, HALO : HALO + rows, :] + in_o[ch]
        for at, strip, corner in zip(ends(rows - HALO), (first, second), (c_first, c_second)):
            buf[ch, pl.ds(at, HALO)] += strip[ch, b] + corner[ch]
    lanes = pl.ds(pl.multiple_of(b * LANE, LANE), LANE)
    cp = pltpu.make_async_copy(buf, out.at[:, :, lanes], sem.at[0])
    cp.start()
    cp.wait()


def call(kernel, in_specs, out_specs, out_shape, scratch=(), limit=8 << 20, flops=0, moved=0, aliases=None):
    return pl.pallas_call(
        kernel,
        in_specs=in_specs,
        out_specs=out_specs,
        out_shape=out_shape,
        scratch_shapes=scratch,
        input_output_aliases=aliases or {},
        compiler_params=pltpu.CompilerParams(vmem_limit_bytes=limit),
        cost_estimate=pl.CostEstimate(flops=flops, bytes_accessed=moved, transcendentals=0),
    )


def shift(array, axis, pairs):
    return lax.ppermute(array, axis, pairs)


def program(object_field, probe, positions, frame_count, measured):
    width = probe.shape[-1]
    modes = probe.shape[0]
    _, rows, cols = object_field.shape
    blocks = cols // LANE
    n_gx = lax.axis_size("gx")
    n_gy = lax.axis_size("gy")
    slots = measured.shape[2]
    info = jnp.concatenate([frame_count.reshape(1), positions.reshape(2 * slots)]).reshape(1, -1)
    object_field, probe, measured = [pltpu.with_memory_space_constraint(a, pltpu.HBM) for a in (object_field, probe, measured[0, 0])]
    pairs_e = [(i, i ^ 1) for i in range(n_gx) if i ^ 1 < n_gx]
    pairs_o = [(i, i + 1) for i in range(1, n_gx - 1, 2)]
    pairs_o += [(j, i) for i, j in pairs_o]
    pairs_1 = [(i, i ^ 1) for i in range(n_gy) if i ^ 1 < n_gy]
    pairs_2 = [(i, i + 1) for i in range(1, n_gy - 1, 2)]
    pairs_2 += [(j, i) for i, j in pairs_2]

    def diagonal(pairs):
        return [(i * n_gy + z, j * n_gy + w) for z, w in pairs for i, j in pairs_o]

    shape = functools.partial(jax.ShapeDtypeStruct, dtype=F32)
    vmem = pltpu.VMEM
    dma = pltpu.SemaphoreType.DMA
    big, small = [pltpu.with_memory_space_constraint(a, pltpu.HBM) for a in dft_tables(width)]

    strip = shape((2, HALO, cols))
    edge = shape((2, rows, HALO))
    first, second = call(rows_kernel, [HB], [VM] * 2, [strip] * 2, [dma((2,))])(object_field)
    first = shift(first, "gy", pairs_1)
    second = shift(second, "gy", pairs_2)
    in_o = shift(call(outer_edge_kernel, [HB], VM, edge, [dma((1,))])(object_field), "gx", pairs_o)
    in_e = shift(call(inner_edge_kernel, [HB], VM, edge, [dma((1,))])(object_field), "gx", pairs_e)

    ext_shape = (2, blocks + 2, rows + 2 * HALO, LANE)
    amp, ext, acc, probe, big, small = call(
        prepare_kernel,
        [SM] + [HB] * 5,
        [VM] * 6,
        [shape(measured.shape), shape(ext_shape), shape(ext_shape), shape(probe.shape),
         jax.ShapeDtypeStruct(big.shape, BF16), jax.ShapeDtypeStruct(small.shape, BF16)],
        [vmem(measured.shape, F32), dma((4 + blocks,))],
        limit=24 << 20,
        flops=10**9,
        moved=10**7,
    )(info, measured, object_field, probe, big, small)

    corner = shape((2, 2, HALO, HALO))
    corner_e, corner_o = call(corners_kernel, [VM] * 2, [VM] * 2, [corner] * 2)(first, second)
    c_e = shift(corner_e, "gx", pairs_e)
    c_o = shift(corner_o, "gx", pairs_o)

    work = [
        vmem((2, width, width), F32),
        vmem((modes, width, 2 * width), BF16),
        vmem((modes, 2 * width, width), BF16),
        vmem((modes, width, width), BF16),
        vmem((modes, width, width), BF16),
        vmem((modes, width, width), BF16),
        vmem((modes, width, width), BF16),
        vmem((modes, 2, width, width), F32),
        vmem((2, width // 2, width), F32),
    ]
    ext, acc = call(
        near_kernel,
        [SM] + [VM] * 10,
        [VM] * 2,
        [shape(ext_shape)] * 2,
        work,
        limit=32 << 20,
        flops=10**10,
        moved=10**7,
        aliases={9: 0, 10: 1},
    )(info, first, second, in_e, c_e, probe, amp, big, small, ext, acc)
    piece = shape((2, HALO, HALO))
    _, acc, rim_e, rim_o, rim_1, rim_2 = call(
        outer_kernel,
        [SM] + [VM] * 8,
        [VM] * 6,
        [shape(ext_shape)] * 2 + [shape((2, rows + 2 * HALO, HALO)), edge, piece, piece],
        work,
        limit=32 << 20,
        flops=10**10,
        moved=10**7,
        aliases={7: 0, 8: 1},
    )(info, in_o, c_o, probe, amp, big, small, ext, acc)

    back_e = shift(rim_e, "gx", pairs_e)
    back_o = shift(rim_o, "gx", pairs_o)
    strip = shape((2, blocks, HALO, LANE))
    first, second = call(rims_kernel, [VM] * 2, [VM] * 2, [strip] * 2)(acc, back_e)
    first = shift(first, "gy", pairs_1)
    second = shift(second, "gy", pairs_2)
    c_first = shift(rim_1, ("gx", "gy"), diagonal(pairs_1))
    c_second = shift(rim_2, ("gx", "gy"), diagonal(pairs_2))
    whole = shape(object_field.shape)
    out = call(
        inner_join_kernel,
        [VM] * 4,
        HB,
        whole,
        [vmem((2, blocks - 1, rows, LANE), F32), dma((blocks - 1,))],
    )(acc, back_e, first, second)
    return call(
        outer_join_kernel,
        [VM] * 6 + [HB],
        HB,
        whole,
        [vmem((2, rows, LANE), F32), dma((1,))],
        aliases={6: 0},
    )(acc, back_o, first, second, c_first, c_second, out)


def solution(mesh):
    return jax.shard_map(
        program,
        mesh=mesh,
        in_specs=(
            P(None, "gy", "gx"),
            P(),
            P("gy", "gx", None, None),
            P("gy", "gx"),
            P("gy", "gx", None, None, None),
        ),
        out_specs=P(None, "gy", "gx"),
        check_vma=False,
    )
```

```python
import functools
import math

import jax
import jax.numpy as jnp
import numpy as np
from jax import lax
from jax.experimental import pallas as pl
from jax.experimental.pallas import tpu as pltpu
from jax.sharding import PartitionSpec as P


HALO = 128
LANE = 128
F32 = jnp.float32
BF16 = jnp.bfloat16
ANY = pl.BlockSpec(memory_space=pl.ANY)
VM = pl.BlockSpec(memory_space=pltpu.VMEM)
SM = pl.BlockSpec(memory_space=pltpu.SMEM)
HB = pl.BlockSpec(memory_space=pltpu.HBM)


def dft_tables(width):
    half = width // 2
    t = np.arange(width)
    order = np.concatenate([t[0::2], t[1::2]])
    phase = 2.0 * math.pi / width * np.mod(np.outer(t, order), width)
    c = np.cos(phase) / math.sqrt(width)
    s = np.sin(phase) / math.sqrt(width)
    blocks, small = [], []
    for b in (slice(0, half), slice(half, width)):
        blocks += [np.concatenate([c[:, b], s[:, b]]), np.concatenate([-s[:, b], c[:, b]])]
        ct, st = c[:half, b].T, s[:half, b].T
        small.append(np.block([[ct, st], [-st, ct]]))
    fwd = np.concatenate(blocks, axis=1)
    big = np.stack([fwd, fwd.T])
    small = np.stack(small + [m.T for m in small])
    return jnp.asarray(big, BF16), jnp.asarray(small, BF16)


def dot(a, b):
    return jnp.dot(a, b, preferred_element_type=F32)


def sides(blocks):
    odd = lax.rem(lax.axis_index("gx"), 2) == 1
    return jnp.where(odd, 0, blocks + 1), jnp.where(odd, blocks + 1, 0)


def ends(far):
    odd = lax.rem(lax.axis_index("gy"), 2) == 1
    first, second = jnp.where(odd, 0, far), jnp.where(odd, far, 0)
    return pl.multiple_of(first, HALO), pl.multiple_of(second, HALO)


def rows_kernel(own, first, second, sem):
    offsets = ends(own.shape[1] - HALO)
    copies = [
        pltpu.make_async_copy(own.at[:, pl.ds(at, HALO), :], strip, sem.at[i])
        for i, (at, strip) in enumerate(zip(offsets, (first, second)))
    ]
    for cp in copies:
        cp.start()
    for cp in copies:
        cp.wait()


def edge_kernel(which, own, edge, sem):
    block = sides(own.shape[2] // LANE - 2)[which]
    lanes = pl.ds(pl.multiple_of(block * LANE, LANE), LANE)
    cp = pltpu.make_async_copy(own.at[:, :, lanes], edge, sem.at[0])
    cp.start()
    cp.wait()


def inner_edge_kernel(*refs):
    edge_kernel(0, *refs)


def outer_edge_kernel(*refs):
    edge_kernel(1, *refs)


def corners_kernel(first, second, corner_e, corner_o):
    block_e, block_o = sides(first.shape[2] // LANE - 2)
    for i, strip in enumerate((first, second)):
        corner_e[i] = strip[:, :, pl.ds(pl.multiple_of(block_e * LANE, LANE), LANE)]
        corner_o[i] = strip[:, :, pl.ds(pl.multiple_of(block_o * LANE, LANE), LANE)]


def prepare_kernel(pos, count, measured_h, own, probe, big, small, amp, ext, acc, probe_v, big_v, small_v, measured, sem):
    slots, width, _ = measured.shape
    half = width // 2
    rows = own.shape[1]
    blocks = own.shape[2] // LANE
    copies = [(measured_h, measured), (probe, probe_v), (big, big_v), (small, small_v)]
    for b in range(blocks):
        copies.append((own.at[:, :, pl.ds(b * LANE, LANE)], ext.at[:, b + 1, pl.ds(HALO, rows)]))
    copies = [pltpu.make_async_copy(p, q, sem.at[i]) for i, (p, q) in enumerate(copies)]
    for cp in copies:
        cp.start()
    acc[...] = jnp.zeros_like(acc)
    i = lax.broadcasted_iota(jnp.int32, (width, width), 0)
    j = lax.broadcasted_iota(jnp.int32, (width, width), 1)
    source = jnp.where(j < half, 2 * j, 2 * (j - half) + 1)
    cols = (i == source).astype(F32)
    source = jnp.where(i < half, 2 * i, 2 * (i - half) + 1)
    perm = (j == source).astype(F32)
    copies[0].wait()
    for k in range(slots):
        a = jnp.sqrt(measured[k])
        a = jnp.dot(perm, a, precision=lax.Precision.HIGHEST, preferred_element_type=F32)
        amp[k] = jnp.dot(a, cols, precision=lax.Precision.HIGHEST, preferred_element_type=F32)
    for cp in copies[1:]:
        cp.wait()


def one_frame(slot, pos, ext, acc, probe, amp, big, small, patch, x, y, xa, xb, u, v, wave, factor):
    modes, _, width, _ = probe.shape
    h = width // 2
    chunk = 64
    lo, hi = slice(0, h), slice(h, width)
    r = pos[0, slot]
    c = pos[1, slot]
    q = jnp.minimum(c // LANE, ext.shape[1] - 3)
    s = c - q * LANE
    left = jnp.bitwise_and(LANE - s, LANE - 1)
    right = jnp.bitwise_and(s, LANE - 1)
    lane = lax.broadcasted_iota(jnp.int32, (chunk, LANE), 1)
    keep = lane < LANE - s
    for ch in range(2):
        for i in range(0, width, chunk):
            rows = pl.ds(r + i, chunk)
            rot = [pltpu.roll(ext[ch, q + t, rows, :], left, 1) for t in range(3)]
            patch[ch, i : i + chunk, lo] = jnp.where(keep, rot[0], rot[1])
            patch[ch, i : i + chunk, hi] = jnp.where(keep, rot[1], rot[2])
    for m in range(modes):
        for i in range(0, width, chunk):
            rows = slice(i, i + chunk)
            for cc in (lo, hi):
                pr, pi = probe[m, 0, rows, cc], probe[m, 1, rows, cc]
                o_re, o_im = patch[0, rows, cc], patch[1, rows, cc]
                x[m, rows, cc] = (pr * o_re - pi * o_im).astype(BF16)
                x[m, rows, slice(width + cc.start, width + cc.stop)] = (pr * o_im + pi * o_re).astype(BF16)
        for k in range(2):
            e = dot(x[m], big[0, :, k * width : (k + 1) * width])
            y[m, 0:width, k * h : (k + 1) * h] = e[:, lo].astype(BF16)
            y[m, width:, k * h : (k + 1) * h] = e[:, hi].astype(BF16)
    for m in range(modes):
        for k in range(2):
            p = dot(big[1, k * width : (k + 1) * width], y[m])
            wave[m, k] = p
            square = p[lo] * p[lo] + p[hi] * p[hi]
            factor[k] = square if m == 0 else factor[k] + square
    for k in range(2):
        factor[k] = 1.0 - amp[slot, k * h : (k + 1) * h, :] * lax.rsqrt(factor[k] + 1.0)
    for m in range(modes):
        for k in range(2):
            f = factor[k]
            for part in (lo, hi):
                w = f * wave[m, k, part, :]
                xa[m, k * h : (k + 1) * h, part] = w[:, lo].astype(BF16)
                xb[m, k * h : (k + 1) * h, part] = w[:, hi].astype(BF16)
    for m in range(modes):
        a, b = dot(xa[m], small[0]), dot(xb[m], small[1])
        for cc, z in ((lo, a + b), (hi, a - b)):
            for part in (lo, hi):
                u[m, part, cc] = z[lo, part].astype(BF16)
                v[m, part, cc] = z[hi, part].astype(BF16)
    for m in range(modes):
        a, b = dot(small[2], u[m]), dot(small[3], v[m])
        for rows, z in ((lo, a + b), (hi, a - b)):
            pr, pi = probe[m, 0, rows, :], probe[m, 1, rows, :]
            g_re = pr * z[lo] + pi * z[hi]
            g_im = pr * z[hi] - pi * z[lo]
            if m > 0:
                g_re = g_re + patch[0, rows, :]
                g_im = g_im + patch[1, rows, :]
            patch[0, rows, :] = g_re
            patch[1, rows, :] = g_im
    first = lane < s
    for ch in range(2):
        for i in range(0, width, chunk):
            rows = pl.ds(r + i, chunk)
            g0 = pltpu.roll(patch[ch, i : i + chunk, lo], right, 1)
            g1 = pltpu.roll(patch[ch, i : i + chunk, hi], right, 1)
            zero = jnp.zeros_like(g0)
            acc[ch, q, rows, :] += jnp.where(first, zero, g0)
            acc[ch, q + 1, rows, :] += jnp.where(first, g0, g1)
            acc[ch, q + 2, rows, :] += jnp.where(first, g1, zero)


def frame_stage(slot, pos, cols, width):
    c = pos[1, slot]
    odd = lax.rem(lax.axis_index("gx"), 2) == 1
    return jnp.where(odd, c > cols + HALO - width, c < HALO).astype(jnp.int32)


def run_frames(stage, pos, count, ext, acc, probe, amp, big, small, *scratch):
    width = probe.shape[-1]
    cols = (ext.shape[1] - 2) * LANE

    def step(slot, carry):
        @pl.when(frame_stage(slot, pos, cols, width) == stage)
        def _():
            one_frame(slot, pos, ext, acc, probe, amp, big, small, *scratch)

        return carry

    lax.fori_loop(0, count[0, 0], step, 0)


def near_kernel(pos, count, first, second, in_e, c_e, probe, amp, big, small, ext_in, acc_in, ext, acc, *rest):
    blocks = ext.shape[1] - 2
    rows = ext.shape[2] - 2 * HALO
    col_e, _ = sides(blocks)
    for i, (at, strip) in enumerate(zip(ends(HALO + rows), (first, second))):
        for ch in range(2):
            for b in range(blocks):
                ext[ch, b + 1, pl.ds(at, HALO)] = strip[ch, :, b * LANE : (b + 1) * LANE]
            ext[ch, col_e, pl.ds(at, HALO)] = c_e[i, ch]
    for ch in range(2):
        ext[ch, col_e, HALO : HALO + rows] = in_e[ch]
    run_frames(0, pos, count, ext, acc, probe, amp, big, small, *rest)


def outer_kernel(pos, count, in_o, c_o, probe, amp, big, small, ext_in, acc_in,
                 ext, acc, rim_e, rim_o, rim_first, rim_second, *rest):
    blocks = ext.shape[1] - 2
    rows = ext.shape[2] - 2 * HALO
    col_e, col_o = sides(blocks)
    offsets = ends(HALO + rows)
    for ch in range(2):
        for i, at in enumerate(offsets):
            ext[ch, col_o, pl.ds(at, HALO)] = c_o[i, ch]
        ext[ch, col_o, HALO : HALO + rows] = in_o[ch]
    run_frames(1, pos, count, ext, acc, probe, amp, big, small, *rest)
    for ch in range(2):
        rim_e[ch] = acc[ch, col_e]
        for at, rim in zip(offsets, (rim_first, rim_second)):
            rim[ch] = acc[ch, col_o, pl.ds(at, HALO)]
        rim_o[ch] = acc[ch, col_o, HALO : HALO + rows]


def rims_kernel(acc, in_e, first, second):
    blocks = acc.shape[1] - 2
    block_e, _ = sides(blocks - 2)
    for at, strip in zip(ends(acc.shape[2] - HALO), (first, second)):
        for ch in range(2):
            for b in range(blocks):
                strip[ch, b] = acc[ch, b + 1, pl.ds(at, HALO)]
            strip[ch, block_e] += in_e[ch, pl.ds(at, HALO)]


def inner_join_kernel(acc, in_e, first, second, out, buf, sem):
    blocks = acc.shape[1] - 2
    rows = acc.shape[2] - 2 * HALO
    block_e, block_o = sides(blocks - 2)
    start = jnp.where(block_o == 0, 1, 0)
    copies = []
    for t in range(blocks - 1):
        b = start + t
        for ch in range(2):
            buf[ch, t] = acc[ch, b + 1, HALO : HALO + rows, :]
            for at, strip in zip(ends(rows - HALO), (first, second)):
                buf[ch, t, pl.ds(at, HALO)] += strip[ch, b]
    for ch in range(2):
        buf[ch, block_e - start] += in_e[ch, HALO : HALO + rows]
    for t in range(blocks - 1):
        lanes = pl.ds(pl.multiple_of((start + t) * LANE, LANE), LANE)
        copies.append(pltpu.make_async_copy(buf.at[:, t], out.at[:, :, lanes], sem.at[t]))
        copies[-1].start()
    for cp in copies:
        cp.wait()


def outer_join_kernel(acc, in_o, first, second, c_first, c_second, out_in, out, buf, sem):
    blocks = acc.shape[1] - 2
    rows = acc.shape[2] - 2 * HALO
    _, b = sides(blocks - 2)
    for ch in range(2):
        buf[ch] = acc[ch, b + 1, HALO : HALO + rows, :] + in_o[ch]
        for at, strip, corner in zip(ends(rows - HALO), (first, second), (c_first, c_second)):
            buf[ch, pl.ds(at, HALO)] += strip[ch, b] + corner[ch]
    lanes = pl.ds(pl.multiple_of(b * LANE, LANE), LANE)
    cp = pltpu.make_async_copy(buf, out.at[:, :, lanes], sem.at[0])
    cp.start()
    cp.wait()


def call(kernel, in_specs, out_specs, out_shape, scratch=(), limit=8 << 20, flops=0, moved=0, aliases=None):
    return pl.pallas_call(
        kernel,
        in_specs=in_specs,
        out_specs=out_specs,
        out_shape=out_shape,
        scratch_shapes=scratch,
        input_output_aliases=aliases or {},
        compiler_params=pltpu.CompilerParams(vmem_limit_bytes=limit),
        cost_estimate=pl.CostEstimate(flops=flops, bytes_accessed=moved, transcendentals=0),
    )


def shift(array, axis, pairs):
    return lax.ppermute(array, axis, pairs)


def program(object_field, probe, positions, frame_count, measured):
    width = probe.shape[-1]
    modes = probe.shape[0]
    _, rows, cols = object_field.shape
    blocks = cols // LANE
    n_gx = lax.axis_size("gx")
    n_gy = lax.axis_size("gy")
    slots = measured.shape[2]
    pos = jnp.swapaxes(positions, 2, 3).reshape(2, slots)
    object_field, probe, measured = [pltpu.with_memory_space_constraint(a, pltpu.HBM) for a in (object_field, probe, measured[0, 0])]
    pairs_e = [(i, i ^ 1) for i in range(n_gx) if i ^ 1 < n_gx]
    pairs_o = [(i, i + 1) for i in range(1, n_gx - 1, 2)]
    pairs_o += [(j, i) for i, j in pairs_o]
    pairs_1 = [(i, i ^ 1) for i in range(n_gy) if i ^ 1 < n_gy]
    pairs_2 = [(i, i + 1) for i in range(1, n_gy - 1, 2)]
    pairs_2 += [(j, i) for i, j in pairs_2]

    def diagonal(pairs):
        return [(i * n_gy + z, j * n_gy + w) for z, w in pairs for i, j in pairs_o]

    shape = functools.partial(jax.ShapeDtypeStruct, dtype=F32)
    vmem = pltpu.VMEM
    dma = pltpu.SemaphoreType.DMA
    big, small = [pltpu.with_memory_space_constraint(a, pltpu.HBM) for a in dft_tables(width)]

    strip = shape((2, HALO, cols))
    edge = shape((2, rows, HALO))
    first, second = call(rows_kernel, [HB], [VM] * 2, [strip] * 2, [dma((2,))])(object_field)
    first = shift(first, "gy", pairs_1)
    second = shift(second, "gy", pairs_2)
    in_o = shift(call(outer_edge_kernel, [HB], VM, edge, [dma((1,))])(object_field), "gx", pairs_o)
    in_e = shift(call(inner_edge_kernel, [HB], VM, edge, [dma((1,))])(object_field), "gx", pairs_e)

    ext_shape = (2, blocks + 2, rows + 2 * HALO, LANE)
    amp, ext, acc, probe, big, small = call(
        prepare_kernel,
        [SM] * 2 + [HB] * 5,
        [VM] * 6,
        [shape(measured.shape), shape(ext_shape), shape(ext_shape), shape(probe.shape),
         jax.ShapeDtypeStruct(big.shape, BF16), jax.ShapeDtypeStruct(small.shape, BF16)],
        [vmem(measured.shape, F32), dma((4 + blocks,))],
        limit=24 << 20,
        flops=10**9,
        moved=10**7,
    )(pos, frame_count, measured, object_field, probe, big, small)

    corner = shape((2, 2, HALO, HALO))
    corner_e, corner_o = call(corners_kernel, [VM] * 2, [VM] * 2, [corner] * 2)(first, second)
    c_e = shift(corner_e, "gx", pairs_e)
    c_o = shift(corner_o, "gx", pairs_o)

    work = [
        vmem((2, width, width), F32),
        vmem((modes, width, 2 * width), BF16),
        vmem((modes, 2 * width, width), BF16),
        vmem((modes, width, width), BF16),
        vmem((modes, width, width), BF16),
        vmem((modes, width, width), BF16),
        vmem((modes, width, width), BF16),
        vmem((modes, 2, width, width), F32),
        vmem((2, width // 2, width), F32),
    ]
    ext, acc = call(
        near_kernel,
        [SM] * 2 + [VM] * 10,
        [VM] * 2,
        [shape(ext_shape)] * 2,
        work,
        limit=32 << 20,
        flops=10**10,
        moved=10**7,
        aliases={10: 0, 11: 1},
    )(pos, frame_count, first, second, in_e, c_e, probe, amp, big, small, ext, acc)
    piece = shape((2, HALO, HALO))
    _, acc, rim_e, rim_o, rim_1, rim_2 = call(
        outer_kernel,
        [SM] * 2 + [VM] * 8,
        [VM] * 6,
        [shape(ext_shape)] * 2 + [shape((2, rows + 2 * HALO, HALO)), edge, piece, piece],
        work,
        limit=32 << 20,
        flops=10**10,
        moved=10**7,
        aliases={8: 0, 9: 1},
    )(pos, frame_count, in_o, c_o, probe, amp, big, small, ext, acc)

    back_e = shift(rim_e, "gx", pairs_e)
    back_o = shift(rim_o, "gx", pairs_o)
    strip = shape((2, blocks, HALO, LANE))
    first, second = call(rims_kernel, [VM] * 2, [VM] * 2, [strip] * 2)(acc, back_e)
    first = shift(first, "gy", pairs_1)
    second = shift(second, "gy", pairs_2)
    c_first = shift(rim_1, ("gx", "gy"), diagonal(pairs_1))
    c_second = shift(rim_2, ("gx", "gy"), diagonal(pairs_2))
    whole = shape(object_field.shape)
    out = call(
        inner_join_kernel,
        [VM] * 4,
        HB,
        whole,
        [vmem((2, blocks - 1, rows, LANE), F32), dma((blocks - 1,))],
    )(acc, back_e, first, second)
    return call(
        outer_join_kernel,
        [VM] * 6 + [HB],
        HB,
        whole,
        [vmem((2, rows, LANE), F32), dma((1,))],
        aliases={6: 0},
    )(acc, back_o, first, second, c_first, c_second, out)


def solution(mesh):
    return jax.shard_map(
        program,
        mesh=mesh,
        in_specs=(
            P(None, "gy", "gx"),
            P(),
            P("gy", "gx", None, None),
            P("gy", "gx"),
            P("gy", "gx", None, None, None),
        ),
        out_specs=P(None, "gy", "gx"),
        check_vma=False,
    )
```

```python
import functools
import math

import jax
import jax.numpy as jnp
import numpy as np
from jax import lax
from jax.experimental import pallas as pl
from jax.experimental.pallas import tpu as pltpu
from jax.sharding import PartitionSpec as P


HALO = 128
LANE = 128
F32 = jnp.float32
BF16 = jnp.bfloat16
ANY = pl.BlockSpec(memory_space=pl.ANY)
VM = pl.BlockSpec(memory_space=pltpu.VMEM)
SM = pl.BlockSpec(memory_space=pltpu.SMEM)
HB = pl.BlockSpec(memory_space=pltpu.HBM)


def dft_tables(width):
    half = width // 2
    t = np.arange(width)
    order = np.concatenate([t[0::2], t[1::2]])
    phase = 2.0 * math.pi / width * np.mod(np.outer(t, order), width)
    c = np.cos(phase) / math.sqrt(width)
    s = np.sin(phase) / math.sqrt(width)
    blocks, small = [], []
    for b in (slice(0, half), slice(half, width)):
        blocks += [np.concatenate([c[:, b], s[:, b]]), np.concatenate([-s[:, b], c[:, b]])]
        ct, st = c[:half, b].T, s[:half, b].T
        small.append(np.block([[ct, st], [-st, ct]]))
    fwd = np.concatenate(blocks, axis=1)
    big = np.stack([fwd, fwd.T])
    small = np.stack(small + [m.T for m in small])
    return jnp.asarray(big, BF16), jnp.asarray(small, BF16)


def dot(a, b):
    return jnp.dot(a, b, preferred_element_type=F32)


def sides(blocks):
    odd = lax.rem(lax.axis_index("gx"), 2) == 1
    return jnp.where(odd, 0, blocks + 1), jnp.where(odd, blocks + 1, 0)


def ends(far):
    odd = lax.rem(lax.axis_index("gy"), 2) == 1
    first, second = jnp.where(odd, 0, far), jnp.where(odd, far, 0)
    return pl.multiple_of(first, HALO), pl.multiple_of(second, HALO)


def rows_kernel(own, first, second, sem):
    offsets = ends(own.shape[1] - HALO)
    copies = [
        pltpu.make_async_copy(own.at[:, pl.ds(at, HALO), :], strip, sem.at[i])
        for i, (at, strip) in enumerate(zip(offsets, (first, second)))
    ]
    for cp in copies:
        cp.start()
    for cp in copies:
        cp.wait()


def edge_kernel(which, own, edge, sem):
    block = sides(own.shape[2] // LANE - 2)[which]
    lanes = pl.ds(pl.multiple_of(block * LANE, LANE), LANE)
    cp = pltpu.make_async_copy(own.at[:, :, lanes], edge, sem.at[0])
    cp.start()
    cp.wait()


def inner_edge_kernel(*refs):
    edge_kernel(0, *refs)


def outer_edge_kernel(*refs):
    edge_kernel(1, *refs)


def corners_kernel(first, second, corner_e, corner_o):
    block_e, block_o = sides(first.shape[2] // LANE - 2)
    for i, strip in enumerate((first, second)):
        corner_e[i] = strip[:, :, pl.ds(pl.multiple_of(block_e * LANE, LANE), LANE)]
        corner_o[i] = strip[:, :, pl.ds(pl.multiple_of(block_o * LANE, LANE), LANE)]


def prepare_kernel(pos, count, measured_h, own, probe, big, small, amp, ext, acc, probe_v, big_v, small_v, measured, sem):
    slots, width, _ = measured.shape
    half = width // 2
    rows = own.shape[1]
    blocks = own.shape[2] // LANE
    copies = [(measured_h, measured), (probe, probe_v), (big, big_v), (small, small_v)]
    for b in range(blocks):
        copies.append((own.at[:, :, pl.ds(b * LANE, LANE)], ext.at[:, b + 1, pl.ds(HALO, rows)]))
    copies = [pltpu.make_async_copy(p, q, sem.at[i]) for i, (p, q) in enumerate(copies)]
    for cp in copies:
        cp.start()
    acc[...] = jnp.zeros_like(acc)
    i = lax.broadcasted_iota(jnp.int32, (width, width), 0)
    j = lax.broadcasted_iota(jnp.int32, (width, width), 1)
    source = jnp.where(j < half, 2 * j, 2 * (j - half) + 1)
    cols = (i == source).astype(F32)
    source = jnp.where(i < half, 2 * i, 2 * (i - half) + 1)
    perm = (j == source).astype(F32)
    copies[0].wait()
    for k in range(slots):
        a = jnp.sqrt(measured[k])
        a = jnp.dot(perm, a, precision=lax.Precision.HIGHEST, preferred_element_type=F32)
        amp[k] = jnp.dot(a, cols, precision=lax.Precision.HIGHEST, preferred_element_type=F32)
    for cp in copies[1:]:
        cp.wait()


def one_frame(slot, pos, ext, acc, probe, amp, big, small, patch, x, y, xa, xb, u, v, wave, factor):
    modes, _, width, _ = probe.shape
    h = width // 2
    chunk = 64
    lo, hi = slice(0, h), slice(h, width)
    r = pos[0, slot]
    c = pos[1, slot]
    q = jnp.minimum(c // LANE, ext.shape[1] - 3)
    s = c - q * LANE
    left = jnp.bitwise_and(LANE - s, LANE - 1)
    right = jnp.bitwise_and(s, LANE - 1)
    lane = lax.broadcasted_iota(jnp.int32, (chunk, LANE), 1)
    keep = lane < LANE - s
    for ch in range(2):
        for i in range(0, width, chunk):
            rows = pl.ds(r + i, chunk)
            rot = [pltpu.roll(ext[ch, q + t, rows, :], left, 1) for t in range(3)]
            patch[ch, i : i + chunk, lo] = jnp.where(keep, rot[0], rot[1])
            patch[ch, i : i + chunk, hi] = jnp.where(keep, rot[1], rot[2])
    for m in range(modes):
        for i in range(0, width, chunk):
            rows = slice(i, i + chunk)
            for cc in (lo, hi):
                pr, pi = probe[m, 0, rows, cc], probe[m, 1, rows, cc]
                o_re, o_im = patch[0, rows, cc], patch[1, rows, cc]
                x[m, rows, cc] = (pr * o_re - pi * o_im).astype(BF16)
                x[m, rows, slice(width + cc.start, width + cc.stop)] = (pr * o_im + pi * o_re).astype(BF16)
        for k in range(2):
            for i in range(0, width, h):
                e = dot(x[m, i : i + h], big[0, :, k * width : (k + 1) * width])
                y[m, i : i + h, k * h : (k + 1) * h] = e[:, lo].astype(BF16)
                y[m, width + i : width + i + h, k * h : (k + 1) * h] = e[:, hi].astype(BF16)
    for m in range(modes):
        for k in range(2):
            p = dot(big[1, k * width : (k + 1) * width], y[m])
            wave[m, k] = p
            square = p[lo] * p[lo] + p[hi] * p[hi]
            factor[k] = square if m == 0 else factor[k] + square
    for k in range(2):
        factor[k] = 1.0 - amp[slot, k * h : (k + 1) * h, :] * lax.rsqrt(factor[k] + 1.0)
    for m in range(modes):
        for k in range(2):
            f = factor[k]
            for part in (lo, hi):
                w = f * wave[m, k, part, :]
                xa[m, k * h : (k + 1) * h, part] = w[:, lo].astype(BF16)
                xb[m, k * h : (k + 1) * h, part] = w[:, hi].astype(BF16)
    for m in range(modes):
        a, b = dot(xa[m], small[0]), dot(xb[m], small[1])
        for cc, z in ((lo, a + b), (hi, a - b)):
            for part in (lo, hi):
                u[m, part, cc] = z[lo, part].astype(BF16)
                v[m, part, cc] = z[hi, part].astype(BF16)
    for m in range(modes):
        a, b = dot(small[2], u[m]), dot(small[3], v[m])
        for rows, z in ((lo, a + b), (hi, a - b)):
            pr, pi = probe[m, 0, rows, :], probe[m, 1, rows, :]
            g_re = pr * z[lo] + pi * z[hi]
            g_im = pr * z[hi] - pi * z[lo]
            if m > 0:
                g_re = g_re + patch[0, rows, :]
                g_im = g_im + patch[1, rows, :]
            patch[0, rows, :] = g_re
            patch[1, rows, :] = g_im
    first = lane < s
    for ch in range(2):
        for i in range(0, width, chunk):
            rows = pl.ds(r + i, chunk)
            g0 = pltpu.roll(patch[ch, i : i + chunk, lo], right, 1)
            g1 = pltpu.roll(patch[ch, i : i + chunk, hi], right, 1)
            zero = jnp.zeros_like(g0)
            acc[ch, q, rows, :] += jnp.where(first, zero, g0)
            acc[ch, q + 1, rows, :] += jnp.where(first, g0, g1)
            acc[ch, q + 2, rows, :] += jnp.where(first, g1, zero)


def frame_stage(slot, pos, cols, width):
    c = pos[1, slot]
    odd = lax.rem(lax.axis_index("gx"), 2) == 1
    return jnp.where(odd, c > cols + HALO - width, c < HALO).astype(jnp.int32)


def run_frames(stage, pos, count, ext, acc, probe, amp, big, small, *scratch):
    width = probe.shape[-1]
    cols = (ext.shape[1] - 2) * LANE

    def step(slot, carry):
        @pl.when(frame_stage(slot, pos, cols, width) == stage)
        def _():
            one_frame(slot, pos, ext, acc, probe, amp, big, small, *scratch)

        return carry

    lax.fori_loop(0, count[0, 0], step, 0)


def near_kernel(pos, count, first, second, in_e, c_e, probe, amp, big, small, ext_in, acc_in, ext, acc, *rest):
    blocks = ext.shape[1] - 2
    rows = ext.shape[2] - 2 * HALO
    col_e, _ = sides(blocks)
    for i, (at, strip) in enumerate(zip(ends(HALO + rows), (first, second))):
        for ch in range(2):
            for b in range(blocks):
                ext[ch, b + 1, pl.ds(at, HALO)] = strip[ch, :, b * LANE : (b + 1) * LANE]
            ext[ch, col_e, pl.ds(at, HALO)] = c_e[i, ch]
    for ch in range(2):
        ext[ch, col_e, HALO : HALO + rows] = in_e[ch]
    run_frames(0, pos, count, ext, acc, probe, amp, big, small, *rest)


def outer_kernel(pos, count, in_o, c_o, probe, amp, big, small, ext_in, acc_in,
                 ext, acc, rim_e, rim_o, rim_first, rim_second, *rest):
    blocks = ext.shape[1] - 2
    rows = ext.shape[2] - 2 * HALO
    col_e, col_o = sides(blocks)
    offsets = ends(HALO + rows)
    for ch in range(2):
        for i, at in enumerate(offsets):
            ext[ch, col_o, pl.ds(at, HALO)] = c_o[i, ch]
        ext[ch, col_o, HALO : HALO + rows] = in_o[ch]
    run_frames(1, pos, count, ext, acc, probe, amp, big, small, *rest)
    for ch in range(2):
        rim_e[ch] = acc[ch, col_e]
        for at, rim in zip(offsets, (rim_first, rim_second)):
            rim[ch] = acc[ch, col_o, pl.ds(at, HALO)]
        rim_o[ch] = acc[ch, col_o, HALO : HALO + rows]


def rims_kernel(acc, in_e, first, second):
    blocks = acc.shape[1] - 2
    block_e, _ = sides(blocks - 2)
    for at, strip in zip(ends(acc.shape[2] - HALO), (first, second)):
        for ch in range(2):
            for b in range(blocks):
                strip[ch, b] = acc[ch, b + 1, pl.ds(at, HALO)]
            strip[ch, block_e] += in_e[ch, pl.ds(at, HALO)]


def inner_join_kernel(acc, in_e, first, second, out, buf, sem):
    blocks = acc.shape[1] - 2
    rows = acc.shape[2] - 2 * HALO
    block_e, block_o = sides(blocks - 2)
    start = jnp.where(block_o == 0, 1, 0)
    copies = []
    for t in range(blocks - 1):
        b = start + t
        for ch in range(2):
            buf[ch, t] = acc[ch, b + 1, HALO : HALO + rows, :]
            for at, strip in zip(ends(rows - HALO), (first, second)):
                buf[ch, t, pl.ds(at, HALO)] += strip[ch, b]
    for ch in range(2):
        buf[ch, block_e - start] += in_e[ch, HALO : HALO + rows]
    for t in range(blocks - 1):
        lanes = pl.ds(pl.multiple_of((start + t) * LANE, LANE), LANE)
        copies.append(pltpu.make_async_copy(buf.at[:, t], out.at[:, :, lanes], sem.at[t]))
        copies[-1].start()
    for cp in copies:
        cp.wait()


def outer_join_kernel(acc, in_o, first, second, c_first, c_second, out_in, out, buf, sem):
    blocks = acc.shape[1] - 2
    rows = acc.shape[2] - 2 * HALO
    _, b = sides(blocks - 2)
    for ch in range(2):
        buf[ch] = acc[ch, b + 1, HALO : HALO + rows, :] + in_o[ch]
        for at, strip, corner in zip(ends(rows - HALO), (first, second), (c_first, c_second)):
            buf[ch, pl.ds(at, HALO)] += strip[ch, b] + corner[ch]
    lanes = pl.ds(pl.multiple_of(b * LANE, LANE), LANE)
    cp = pltpu.make_async_copy(buf, out.at[:, :, lanes], sem.at[0])
    cp.start()
    cp.wait()


def call(kernel, in_specs, out_specs, out_shape, scratch=(), limit=8 << 20, flops=0, moved=0, aliases=None):
    return pl.pallas_call(
        kernel,
        in_specs=in_specs,
        out_specs=out_specs,
        out_shape=out_shape,
        scratch_shapes=scratch,
        input_output_aliases=aliases or {},
        compiler_params=pltpu.CompilerParams(vmem_limit_bytes=limit),
        cost_estimate=pl.CostEstimate(flops=flops, bytes_accessed=moved, transcendentals=0),
    )


def shift(array, axis, pairs):
    return lax.ppermute(array, axis, pairs)


def program(object_field, probe, positions, frame_count, measured):
    width = probe.shape[-1]
    modes = probe.shape[0]
    _, rows, cols = object_field.shape
    blocks = cols // LANE
    n_gx = lax.axis_size("gx")
    n_gy = lax.axis_size("gy")
    slots = measured.shape[2]
    pos = jnp.swapaxes(positions, 2, 3).reshape(2, slots)
    object_field, probe, measured = [pltpu.with_memory_space_constraint(a, pltpu.HBM) for a in (object_field, probe, measured[0, 0])]
    pairs_e = [(i, i ^ 1) for i in range(n_gx) if i ^ 1 < n_gx]
    pairs_o = [(i, i + 1) for i in range(1, n_gx - 1, 2)]
    pairs_o += [(j, i) for i, j in pairs_o]
    pairs_1 = [(i, i ^ 1) for i in range(n_gy) if i ^ 1 < n_gy]
    pairs_2 = [(i, i + 1) for i in range(1, n_gy - 1, 2)]
    pairs_2 += [(j, i) for i, j in pairs_2]

    def diagonal(pairs):
        return [(i * n_gy + z, j * n_gy + w) for z, w in pairs for i, j in pairs_o]

    shape = functools.partial(jax.ShapeDtypeStruct, dtype=F32)
    vmem = pltpu.VMEM
    dma = pltpu.SemaphoreType.DMA
    big, small = [pltpu.with_memory_space_constraint(a, pltpu.HBM) for a in dft_tables(width)]

    strip = shape((2, HALO, cols))
    edge = shape((2, rows, HALO))
    first, second = call(rows_kernel, [HB], [VM] * 2, [strip] * 2, [dma((2,))])(object_field)
    first = shift(first, "gy", pairs_1)
    second = shift(second, "gy", pairs_2)
    in_o = shift(call(outer_edge_kernel, [HB], VM, edge, [dma((1,))])(object_field), "gx", pairs_o)
    in_e = shift(call(inner_edge_kernel, [HB], VM, edge, [dma((1,))])(object_field), "gx", pairs_e)

    ext_shape = (2, blocks + 2, rows + 2 * HALO, LANE)
    amp, ext, acc, probe, big, small = call(
        prepare_kernel,
        [SM] * 2 + [HB] * 5,
        [VM] * 6,
        [shape(measured.shape), shape(ext_shape), shape(ext_shape), shape(probe.shape),
         jax.ShapeDtypeStruct(big.shape, BF16), jax.ShapeDtypeStruct(small.shape, BF16)],
        [vmem(measured.shape, F32), dma((4 + blocks,))],
        limit=24 << 20,
        flops=10**9,
        moved=10**7,
    )(pos, frame_count, measured, object_field, probe, big, small)

    corner = shape((2, 2, HALO, HALO))
    corner_e, corner_o = call(corners_kernel, [VM] * 2, [VM] * 2, [corner] * 2)(first, second)
    c_e = shift(corner_e, "gx", pairs_e)
    c_o = shift(corner_o, "gx", pairs_o)

    work = [
        vmem((2, width, width), F32),
        vmem((modes, width, 2 * width), BF16),
        vmem((modes, 2 * width, width), BF16),
        vmem((modes, width, width), BF16),
        vmem((modes, width, width), BF16),
        vmem((modes, width, width), BF16),
        vmem((modes, width, width), BF16),
        vmem((modes, 2, width, width), F32),
        vmem((2, width // 2, width), F32),
    ]
    ext, acc = call(
        near_kernel,
        [SM] * 2 + [VM] * 10,
        [VM] * 2,
        [shape(ext_shape)] * 2,
        work,
        limit=32 << 20,
        flops=10**10,
        moved=10**7,
        aliases={10: 0, 11: 1},
    )(pos, frame_count, first, second, in_e, c_e, probe, amp, big, small, ext, acc)
    piece = shape((2, HALO, HALO))
    _, acc, rim_e, rim_o, rim_1, rim_2 = call(
        outer_kernel,
        [SM] * 2 + [VM] * 8,
        [VM] * 6,
        [shape(ext_shape)] * 2 + [shape((2, rows + 2 * HALO, HALO)), edge, piece, piece],
        work,
        limit=32 << 20,
        flops=10**10,
        moved=10**7,
        aliases={8: 0, 9: 1},
    )(pos, frame_count, in_o, c_o, probe, amp, big, small, ext, acc)

    back_e = shift(rim_e, "gx", pairs_e)
    back_o = shift(rim_o, "gx", pairs_o)
    strip = shape((2, blocks, HALO, LANE))
    first, second = call(rims_kernel, [VM] * 2, [VM] * 2, [strip] * 2)(acc, back_e)
    first = shift(first, "gy", pairs_1)
    second = shift(second, "gy", pairs_2)
    c_first = shift(rim_1, ("gx", "gy"), diagonal(pairs_1))
    c_second = shift(rim_2, ("gx", "gy"), diagonal(pairs_2))
    whole = shape(object_field.shape)
    out = call(
        inner_join_kernel,
        [VM] * 4,
        HB,
        whole,
        [vmem((2, blocks - 1, rows, LANE), F32), dma((blocks - 1,))],
    )(acc, back_e, first, second)
    return call(
        outer_join_kernel,
        [VM] * 6 + [HB],
        HB,
        whole,
        [vmem((2, rows, LANE), F32), dma((1,))],
        aliases={6: 0},
    )(acc, back_o, first, second, c_first, c_second, out)


def solution(mesh):
    return jax.shard_map(
        program,
        mesh=mesh,
        in_specs=(
            P(None, "gy", "gx"),
            P(),
            P("gy", "gx", None, None),
            P("gy", "gx"),
            P("gy", "gx", None, None, None),
        ),
        out_specs=P(None, "gy", "gx"),
        check_vma=False,
    )
```
